32 devices in a mesh: seq: 8 (over z, core), tp: 4 (over y, x).
Axes of the slice: x: 2, y: 2, z: 4, core: 2. Of those that a mesh axis runs over, the one named last changes fastest.
Arguments:
- q_heads: bfloat16 [1024, 4096], P('seq', 'tp'), may hold values from -200 to 200
- k_heads: bfloat16 [1024, 4096], P('seq', 'tp'), may hold values from -4 to 4
- v_heads: bfloat16 [1024, 4096], P('seq', 'tp'), may hold values from -5 to 5
- grad_attn: bfloat16 [1024, 4096], P('seq', 'tp'), may hold values from -5 to 5
- attn_out: bfloat16 [1024, 4096], P('seq', 'tp'), may hold values from -5 to 5
- gate_q: bfloat16 [1024, 8192], P('seq', 'tp'), may hold values from -5 to 5
- feat_k: bfloat16 [1024, 8192], P('seq', 'tp'), may hold values from -5 to 5
- feat_v: bfloat16 [1024, 8192], P('seq', 'tp'), may hold values from -5 to 5
- conv_out: bfloat16 [1024, 8192], P('seq', 'tp'), may hold values from -5 to 5
- grad_y: bfloat16 [1024, 8192], P('seq', 'tp'), may hold values from -5 to 5
- filters: float32 [64, 128], replicated, may hold values from -0.5 to 0.5
Outputs:
- grad_q: bfloat16 [1024, 4096], P('seq', 'tp')
- grad_k: bfloat16 [1024, 4096], P('seq', 'tp')
- grad_v: bfloat16 [1024, 4096], P('seq', 'tp')
- grad_gate: bfloat16 [1024, 8192], P('seq', 'tp')
- grad_feat_k: bfloat16 [1024, 8192], P('seq', 'tp')
- grad_feat_v: bfloat16 [1024, 8192], P('seq', 'tp')
- grad_filters: float32 [64, 128], replicated
The draws below stay inside these ranges and needn't reach their ends.
All inputs are finite; a program needn't handle non-finite values.
Results may differ from the reference program's by a relative error of at most 0.014.
Values may be sent and summed in bfloat16 or wider, within the bound.
A program may use at most 64 MiB of HBM per device.

```python
import math
import jax
import jax.numpy as jnp
from jax import lax

D = 8192
HEADS = 32
DH = 128
GROUPS = 64
FILT = 128
LENGTH = 1024
TOKENS = 1024


def keys_common(key):
    raw = jax.random.normal(jax.random.fold_in(key, 7), (TOKENS, HEADS * DH), jnp.float32)
    return jnp.clip(raw, -4.0, 4.0)


def draw_k_heads(key, part):
    return keys_common(key).astype(jnp.bfloat16)


def draw_q_heads(key, part):
    base = jnp.clip(jax.random.normal(jax.random.fold_in(key, 8), (TOKENS, HEADS * DH), jnp.float32), -4.0, 4.0)
    return base.astype(jnp.bfloat16)


def steps_of(own_key, dims, shards, low, largest):
    def one(dim, shards_of):
        steps = jax.random.uniform(jax.random.fold_in(jax.random.fold_in(own_key, 6), dim), (shards_of,), jnp.float32, low / len(shards), largest / len(shards))
        return jnp.repeat(jnp.exp(steps), dims[dim] // shards_of).reshape((-1,) + (1,) * (len(dims) - dim - 1))

    level = one(*shards[0])
    for cut in shards[1:]:
        level = level * one(*cut)
    return level


def normal_values(stream_key, extent, spread, bound, shards=(), kind=jnp.bfloat16):
    values = jax.random.normal(stream_key, extent, jnp.float32) * spread
    if len(shards) > 0:
        values = steps_of(stream_key, extent, shards, -0.22, 0.18) * values
    return jnp.clip(values, min=-bound, max=bound).astype(kind)


def setup_inputs(seed: int = 0) -> dict:
    seeds = jax.random.split(jax.random.key(seed), 12)
    q_heads = draw_q_heads(jax.random.fold_in(seeds[11], 71), 0)
    k_heads = draw_k_heads(jax.random.fold_in(seeds[11], 71), 0)
    v_heads = normal_values(seeds[2], (TOKENS, HEADS * DH), 1.0, 5.0, ((0, 8), (1, 4)))
    grad_attn = normal_values(seeds[3], (TOKENS, HEADS * DH), 1.0, 5.0, ((0, 8), (1, 4)))
    attn_out = normal_values(seeds[4], (TOKENS, HEADS * DH), 1.0, 5.0, ((0, 8), (1, 4)))
    gate_q = normal_values(seeds[5], (TOKENS, D), 1.0, 5.0, ((0, 8), (1, 4)))
    feat_k = normal_values(seeds[6], (TOKENS, D), 1.0, 5.0, ((0, 8), (1, 4)))
    feat_v = normal_values(seeds[7], (TOKENS, D), 1.0, 5.0, ((0, 8), (1, 4)))
    conv_out = normal_values(seeds[8], (TOKENS, D), 1.0, 5.0, ((0, 8), (1, 4)))
    grad_y = normal_values(seeds[9], (TOKENS, D), 1.0, 5.0, ((0, 8), (1, 4)))
    filters = normal_values(seeds[10], (GROUPS, FILT), FILT ** -0.5, 0.5, (), jnp.float32)
    return {"q_heads": q_heads, "k_heads": k_heads, "v_heads": v_heads, "grad_attn": grad_attn, "attn_out": attn_out, "gate_q": gate_q, "feat_k": feat_k, "feat_v": feat_v, "conv_out": conv_out, "grad_y": grad_y, "filters": filters}


def wire_split(x):
    high = x.astype(jnp.bfloat16)
    back = lax.optimization_barrier(high).astype(jnp.float32)
    low = (x - back).astype(jnp.bfloat16)
    return back + lax.optimization_barrier(low).astype(jnp.float32)


def head_grads(operands):
    query, keyrow, value, upstream, saved = operands
    scale = 1.0 / (DH ** 0.5)
    scores = jnp.dot(query, keyrow.T, preferred_element_type=jnp.float32) * scale
    causal = jnp.arange(LENGTH)[:, None] >= jnp.arange(LENGTH)[None, :]
    masked = jnp.where(causal, scores, -jnp.inf)
    top = jnp.max(masked, axis=1)
    total = jnp.sum(jnp.where(causal, jnp.exp(scores - top[:, None]), 0.0), axis=1)
    lse = top + jnp.log(total)
    probs = jnp.where(causal, jnp.exp(scores - lse[:, None]), 0.0)
    delta = jnp.sum(upstream.astype(jnp.float32) * saved.astype(jnp.float32), axis=1)
    dprob = jnp.dot(upstream, value.T, preferred_element_type=jnp.float32)
    dscore = probs * (dprob - delta[:, None])
    grad_query = jnp.dot(dscore, keyrow.astype(jnp.float32), precision=lax.Precision.HIGHEST) * scale
    lse_w = wire_split(lse)
    delta_w = wire_split(delta)
    probs_k = jnp.where(causal, jnp.exp(scores - lse_w[:, None]), 0.0)
    dscore_k = probs_k * (dprob - delta_w[:, None])
    grad_value = jnp.dot(probs_k.astype(jnp.bfloat16).T, upstream, preferred_element_type=jnp.float32)
    grad_key = jnp.dot(dscore_k.astype(jnp.bfloat16).T, query, preferred_element_type=jnp.float32) * scale
    return grad_query.astype(jnp.bfloat16), grad_key.astype(jnp.bfloat16), grad_value.astype(jnp.bfloat16)


def split_heads(x):
    return x.reshape(LENGTH, HEADS, DH).transpose(1, 0, 2)


def join_heads(x):
    return x.transpose(1, 0, 2).reshape(TOKENS, HEADS * DH)


def conv_block(operands):
    dz_block, mixed_block, taps_block = operands
    length_fft = 2 * LENGTH
    spectrum_dz = jnp.fft.rfft(dz_block, n=length_fft, axis=0)
    spectrum_taps = jnp.fft.rfft(taps_block, n=length_fft, axis=0)
    spectrum_mixed = jnp.fft.rfft(mixed_block, n=length_fft, axis=0)
    dw_block = jnp.fft.irfft(spectrum_dz * jnp.conj(spectrum_taps), n=length_fft, axis=0)[:LENGTH]
    term_block = jnp.fft.irfft(spectrum_dz * jnp.conj(spectrum_mixed), n=length_fft, axis=0)[:FILT]
    return dw_block.astype(dz_block.dtype), term_block.astype(dz_block.dtype)


def reference(q_heads, k_heads, v_heads, grad_attn, attn_out, gate_q, feat_k, feat_v, conv_out, grad_y, filters):
    grad_query, grad_key, grad_value = lax.map(head_grads, (split_heads(q_heads), split_heads(k_heads), split_heads(v_heads), split_heads(grad_attn), split_heads(attn_out)))
    dz = (grad_y.astype(jnp.float32) * gate_q.astype(jnp.float32)).astype(jnp.bfloat16)
    dz = lax.optimization_barrier(dz).astype(jnp.float32)
    grad_gate = (grad_y.astype(jnp.float32) * conv_out.astype(jnp.float32)).astype(jnp.bfloat16)
    taps = filters[jnp.arange(D) % GROUPS].T
    mixed = feat_k.astype(jnp.float32) * feat_v.astype(jnp.float32)
    block_width = math.gcd(D, 1024)
    blocks = D // block_width

    def to_blocks(x):
        return x.reshape(x.shape[0], blocks, block_width).transpose(1, 0, 2)

    dw_blocks, term_blocks = lax.map(conv_block, (to_blocks(dz), to_blocks(mixed), to_blocks(taps)))
    dw = dw_blocks.transpose(1, 0, 2).reshape(LENGTH, D)
    per_channel = term_blocks.transpose(1, 0, 2).reshape(FILT, D)
    columns = jnp.sum(per_channel.reshape(FILT, D // GROUPS, GROUPS), axis=1)
    norm = 1.0 / ((TOKENS * D / GROUPS) ** 0.5)
    grad_filters = columns.T * norm
    grad_feat_k = (dw * feat_v.astype(jnp.float32)).astype(jnp.bfloat16)
    grad_feat_v = (dw * feat_k.astype(jnp.float32)).astype(jnp.bfloat16)
    return (join_heads(grad_query), join_heads(grad_key), join_heads(grad_value), grad_gate, grad_feat_k, grad_feat_v, grad_filters)
```

```python
import functools

import jax
import jax.numpy as jnp
from jax import lax
from jax.experimental import pallas as pl
from jax.experimental.pallas import tpu as pltpu
from jax.sharding import PartitionSpec as P

HEADS = 32


def from_behind(value, axis, steps):
    count = lax.axis_size(axis)
    leading, last = (max(0, -steps), min(count, count - steps))
    return lax.ppermute(value, axis, [(source, source + steps) for source in range(leading, last)])


def wire_parts(x):
    high = x.astype(jnp.bfloat16)
    back = lax.optimization_barrier(high).astype(jnp.float32)
    low = (x - back).astype(jnp.bfloat16)
    return (high, low)


def local_ring(
    q_heads,
    k_heads,
    v_heads,
    grad_attn,
    attn_out,
    gate_q,
    feat_k,
    feat_v,
    conv_out,
    grad_y,
    filters,
):
    rows = q_heads.shape[0]
    heads_here = HEADS // lax.axis_size("tp")
    width = q_heads.shape[1] // heads_here
    scale = 1.0 / width**0.5
    shards = lax.axis_size("seq")
    place = lax.axis_index("seq")
    queries = q_heads.reshape(rows, heads_here, width)
    upstream = grad_attn.reshape(rows, heads_here, width)
    keys_here = k_heads.reshape(rows, heads_here, width)
    values_here = v_heads.reshape(rows, heads_here, width)
    delta = jnp.sum(
        upstream.astype(jnp.float32)
        * attn_out.reshape(rows, heads_here, width).astype(jnp.float32),
        axis=2,
    )
    delta_heads = delta.T
    diagonal = jnp.arange(rows)[:, None] >= jnp.arange(rows)[None, :]

    def query_tile(state, key_piece, value_piece, live):
        top, total, acc = state
        count = key_piece.shape[0]
        key_block = key_piece.reshape(count, heads_here, width)
        value_block = value_piece.reshape(count, heads_here, width)
        scores = (
            jnp.einsum("qhd,khd->hqk", queries, key_block, preferred_element_type=jnp.float32)
            * scale
        )
        top_new = jnp.maximum(top, jnp.max(jnp.where(live[None], scores, -1e30), axis=2))
        weights = jnp.where(live[None], jnp.exp(scores - top_new[:, :, None]), 0.0)
        decay = jnp.exp(top - top_new)
        dprob = jnp.einsum(
            "qhd,khd->hqk", upstream, value_block, preferred_element_type=jnp.float32
        )
        term = jnp.einsum(
            "hqk,khd->qhd",
            weights * (dprob - delta_heads[:, :, None]),
            key_block.astype(jnp.float32),
            precision=lax.Precision.HIGHEST,
        )
        return (top_new, total * decay + jnp.sum(weights, axis=2), acc * decay.T[:, :, None] + term)

    zero_rows = jnp.zeros((rows, heads_here, width), jnp.float32)
    state = (
        jnp.full((heads_here, rows), -1e30, jnp.float32),
        jnp.zeros((heads_here, rows), jnp.float32),
        zero_rows,
    )
    state = query_tile(state, k_heads, v_heads, diagonal)

    def relay_keys(back, carry):
        inner, moving = carry
        moving = from_behind((moving[0], moving[1]), "seq", 1)
        valid = place >= back
        live = jnp.broadcast_to(valid, (rows, rows))
        inner = query_tile(inner, moving[0], moving[1], live)
        return (inner, moving)

    state, moved = lax.fori_loop(1, shards, relay_keys, (state, (k_heads, v_heads)))
    top, total, acc = state
    lse = (top + jnp.log(total)).T
    grad_query = acc * (1.0 / total).T[:, :, None] * scale
    lse_high, lse_low = wire_parts(lse)
    delta_high, delta_low = wire_parts(delta)
    stats = jnp.stack([lse_high, lse_low, delta_high, delta_low], axis=1)

    def key_tile(inner, query_piece, upstream_piece, stat_piece, live):
        key_grad, value_grad = inner
        count = query_piece.shape[0]
        query_block = query_piece.reshape(count, heads_here, width)
        upstream_block = upstream_piece.reshape(count, heads_here, width)
        lse_w = stat_piece[:, 0].astype(jnp.float32) + stat_piece[:, 1].astype(jnp.float32)
        delta_w = stat_piece[:, 2].astype(jnp.float32) + stat_piece[:, 3].astype(jnp.float32)
        scores = (
            jnp.einsum("qhd,khd->hqk", query_block, keys_here, preferred_element_type=jnp.float32)
            * scale
        )
        probs = jnp.where(live[None], jnp.exp(scores - lse_w.T[:, :, None]), 0.0)
        dprob = jnp.einsum(
            "qhd,khd->hqk", upstream_block, values_here, preferred_element_type=jnp.float32
        )
        dscore = probs * (dprob - delta_w.T[:, :, None])
        value_grad = value_grad + jnp.einsum(
            "hqk,qhd->khd",
            probs.astype(jnp.bfloat16),
            upstream_block,
            preferred_element_type=jnp.float32,
        )
        key_grad = key_grad + jnp.einsum(
            "hqk,qhd->khd",
            dscore.astype(jnp.bfloat16),
            query_block,
            preferred_element_type=jnp.float32,
        )
        return (key_grad, value_grad)

    grads = (zero_rows, zero_rows)
    grads = key_tile(grads, q_heads, grad_attn, stats, diagonal)

    def relay_queries(back, carry):
        inner, moving = carry
        moving = from_behind((moving[0], moving[1], moving[2]), "seq", -1)
        valid = place + back <= shards - 1
        live = jnp.broadcast_to(valid, (rows, rows))
        inner = key_tile(inner, moving[0], moving[1], moving[2], live)
        return (inner, moving)

    grads, moved = lax.fori_loop(1, shards, relay_queries, (grads, (q_heads, grad_attn, stats)))
    key_grad, value_grad = grads
    grad_q = grad_query.astype(jnp.bfloat16).reshape(rows, heads_here * width)
    grad_k = (key_grad * scale).astype(jnp.bfloat16).reshape(rows, heads_here * width)
    grad_v = value_grad.astype(jnp.bfloat16).reshape(rows, heads_here * width)
    span_taps = filters.shape[1]
    groups = filters.shape[0]
    channels = gate_q.shape[1]
    dz = (grad_y.astype(jnp.float32) * gate_q.astype(jnp.float32)).astype(jnp.bfloat16)
    rim = from_behind(dz[: span_taps - 1], "seq", -1)
    grad_gate = (grad_y.astype(jnp.float32) * conv_out.astype(jnp.float32)).astype(jnp.bfloat16)
    padded = jnp.concatenate([dz, rim], axis=0).astype(jnp.float32)
    taps = jnp.tile(filters.T, (1, channels // groups))
    mixed = feat_k.astype(jnp.float32) * feat_v.astype(jnp.float32)
    numbers = ("NWC", "WIO", "NWC")
    dw = lax.conv_general_dilated(
        padded[None],
        taps[:, None, :],
        (1,),
        "VALID",
        dimension_numbers=numbers,
        feature_group_count=channels,
        precision=lax.Precision.HIGHEST,
    )[0]
    local_terms = lax.conv_general_dilated(
        padded[None],
        mixed[:, None, :],
        (1,),
        "VALID",
        dimension_numbers=numbers,
        feature_group_count=channels,
        precision=lax.Precision.HIGHEST,
    )[0]
    grad_feat_k = (dw * feat_v.astype(jnp.float32)).astype(jnp.bfloat16)
    grad_feat_v = (dw * feat_k.astype(jnp.float32)).astype(jnp.bfloat16)
    local_terms = jnp.sum(local_terms.reshape(span_taps, channels // groups, groups), axis=1).T
    filter_total = lax.psum(local_terms, ("seq", "tp"))
    count_all = rows * shards * channels * lax.axis_size("tp") / groups
    grad_filters = filter_total * (1.0 / count_all**0.5)
    return (grad_q, grad_k, grad_v, grad_gate, grad_feat_k, grad_feat_v, grad_filters)


MESH = pl.DeviceIdType.MESH
LANES = 128
LOG2E = 1.4426950408889634
CHIPS = 4
CROSS = {0: ((1, 2), (1, 1), (2, 2), (2, 1)), 1: ((1, 2), (2, 2)), 2: ((0, 1), (3, 1)), 3: ((0, 2), (0, 1), (3, 2), (3, 1))}
DELTAS = {2: (1,), 3: (2, 1)}


def kernel(
    n,
    tp,
    q_in,
    k_in,
    v_in,
    do_in,
    ao_in,
    gate_in,
    fk_in,
    fv_in,
    gy_in,
    filters,
    gq_out,
    gk_out,
    gv_out,
    gfk_out,
    gfv_out,
    gf_out,
    heads_q,
    heads_k,
    heads_v,
    heads_do,
    keys_t,
    delta_mine,
    delta_all,
    lse_mine,
    lse_in,
    edge_mine,
    edge_in,
    part_mine,
    part_in,
    do_here,
    ao_here,
    gate,
    fk,
    fv,
    gy,
    dz_here,
    dz_rim,
    dz_all,
    rim_all,
    dw_all,
    taps,
    terms,
    partial_mine,
    partial_in,
    across,
    scores,
    grad_t,
    acc_k,
    acc_v,
    res_q,
    res_k,
    res_v,
    load_sem,
    send_x,
    recv_x,
    send_d,
    recv_d,
    send_l,
    recv_l,
    send_e,
    recv_e,
    send_p,
    recv_p,
    send_rim,
    recv_rim,
    send_out,
    recv_out,
    own_out,
    send_rs,
    recv_rs,
    send_tp,
    recv_tp,
    send_ag,
    recv_ag,
):
    me = lax.axis_index("seq")
    lane = lax.axis_index("tp")
    z = lax.div(me, 2)
    core = lax.rem(me, 2)
    other = 1 - core
    partner = 2 * z + other
    rows, width = q_in.shape[0], LANES
    count = q_in.shape[1] // width // 2
    half = count * width
    tile = 2 * rows
    channels = gy_in.shape[1]
    span = filters.shape[1]
    scale = 1.0 / width**0.5

    def chunk(i, size):
        return pl.ds(pl.multiple_of(i * size, size), size)

    def remote(src, dst, send, recv, device):
        return pltpu.make_async_remote_copy(
            src_ref=src,
            dst_ref=dst,
            send_sem=send,
            recv_sem=recv,
            device_id={"seq": device},
            device_id_type=MESH,
        )

    loads = [
        pltpu.make_async_copy(src, dst, load_sem.at[i])
        for i, (src, dst) in enumerate(
            (
                (do_in, do_here),
                (ao_in, ao_here),
                (gy_in, gy),
                (gate_in, gate),
                (fk_in, fk),
                (fv_in, fv),
            )
        )
    ]
    for load in loads:
        load.start()

    barrier = pltpu.get_barrier_semaphore()
    for d in range(1, n):
        pl.semaphore_signal(
            barrier, inc=1, device_id={"seq": lax.rem(me + d, n)}, device_id_type=MESH
        )
    for d in range(1, tp):
        pl.semaphore_signal(
            barrier, inc=1, device_id={"tp": lax.rem(lane + d, tp)}, device_id_type=MESH
        )
    pl.semaphore_wait(barrier, n - 1 + tp - 1)

    ins = (q_in, k_in, v_in, do_in)
    heads = (heads_q, heads_k, heads_v, heads_do)

    def move(a, h, chip, to):
        return remote(
            ins[a].at[:, chunk(to * count + h, width)],
            heads[a].at[h, chunk(me, rows), :],
            send_x.at[a, chip, to],
            recv_x.at[a, z, h],
            2 * chip + to,
        )

    def moved(a, chip, to):
        return remote(
            ins[a].at[:, chunk(to, half)],
            ins[a].at[:, chunk(to, half)],
            send_x.at[a, chip, to],
            recv_x.at[a, chip, 0],
            2 * chip + to,
        )

    def own(a, h):
        return pltpu.make_async_copy(
            ins[a].at[:, chunk(core * count + h, width)],
            heads[a].at[h, chunk(me, rows), :],
            recv_x.at[a, z, h],
        )

    def arrive(a, chip, h):
        at = heads[a].at[h, chunk(chip, tile), :]
        remote(at, at, send_x.at[a, 0, 0], recv_x.at[a, chip, h], partner).wait_recv()

    def exchange(h):
        for a in (0, 1, 3, 2):
            own(a, h).start()
            move(a, h, z, other).start()

    def outward(h):
        for chip in range(CHIPS):

            @pl.when(z == chip)
            def _():
                for a, to in CROSS[chip]:
                    for side in range(2):
                        move(a, h, to, side).start()

    def rim_copy():
        return remote(dz_here, dz_rim, send_rim, recv_rim, lax.rem(me + n - 1, n))

    def delta_copy(chip, to):
        return remote(
            delta_mine.at[to],
            delta_all.at[me],
            send_d.at[chip, to],
            recv_d.at[me],
            2 * chip + to,
        )

    def delta_wait(chip):
        for side in range(2):
            b = 2 * chip + side
            at = delta_all.at[b]

            @pl.when(b != me)
            def _():
                remote(at, at, send_d.at[0, 0], recv_d.at[b], partner).wait_recv()

    for h in range(count):
        exchange(h)
    outward(0)

    loads[0].wait()
    loads[1].wait()
    for h in range(2 * count):
        at = slice(h * width, (h + 1) * width)
        prod = do_here[:, at].astype(jnp.float32) * ao_here[:, at].astype(jnp.float32)
        line = jnp.sum(prod.T, axis=0, keepdims=True)
        delta_mine[h // count, h % count] = jnp.broadcast_to(line, (8, rows))
    delta_all[me] = delta_mine[core]
    delta_copy(z, other).start()
    for chip, targets in DELTAS.items():

        @pl.when(z == chip)
        def _():
            for to in targets:
                for side in range(2):
                    delta_copy(to, side).start()

    loads[2].wait()
    loads[3].wait()
    tiles = channels // LANES
    for t in range(tiles):
        at = slice(t * LANES, (t + 1) * LANES)
        dz = (gy[:, at].astype(jnp.float32) * gate[:, at].astype(jnp.float32)).astype(jnp.bfloat16)
        dz_here[:, at] = dz
        dz_all[t, 0:rows, :] = dz.astype(jnp.float32)
        dz_all[t, rows : rows + 8, :] = jnp.zeros((8, LANES), jnp.float32)
    outward(1)

    @pl.when(me > 0)
    def _():
        rim_copy().start()

    for h in range(2, count):
        outward(h)

    key_id = lax.broadcasted_iota(jnp.int32, (tile, tile), 0)
    query_id = lax.broadcasted_iota(jnp.int32, (tile, tile), 1)
    nt = (((1,), (1,)), ((), ()))
    nn = (((1,), (0,)), ((), ()))

    def dot(a, b, dims):
        return lax.dot_general(a, b, dims, preferred_element_type=jnp.float32)

    def at_tile(i):
        return slice(i * tile, (i + 1) * tile)

    def log_sums(h, i, keys):
        query = heads_q[h, at_tile(i), :]
        top = None
        for j in keys:
            raw = dot(heads_k[h, at_tile(j), :], query, nt)
            if j == i:
                raw = jnp.where(key_id <= query_id, raw, -1e30)
            scores[at_tile(j), :] = raw
            high = jnp.max(raw, axis=0, keepdims=True)
            top = high if top is None else jnp.maximum(top, high)
        total = jnp.zeros_like(top)
        for j in keys:
            weight = jnp.exp2((scores[at_tile(j), :] - top) * (scale * LOG2E))
            total = total + jnp.sum(weight, axis=0, keepdims=True)
        return top * scale + jnp.log(total)

    def wire(x):
        high = x.astype(jnp.bfloat16).astype(jnp.float32)
        return high + (x - high).astype(jnp.bfloat16).astype(jnp.float32)

    def delta_row(h, i):
        return jnp.concatenate(
            [delta_all[2 * i, h][0:1, :], delta_all[2 * i + 1, h][0:1, :]], axis=1
        )

    def turn_keys(h, j):
        keys_t[:, at_tile(j)] = heads_k[h, at_tile(j), :].T

    def pair(h, i, j, lse, want_q, want_k, fresh_q=False, fresh_k=False):
        query = heads_q[h, at_tile(i), :]
        upstream = heads_do[h, at_tile(i), :]
        delta = delta_row(h, i)
        lse_w = wire(lse)
        base = lse if want_q else lse_w
        raw = dot(heads_k[h, at_tile(j), :], query, nt)
        prob = jnp.exp2(raw * (scale * LOG2E) - base * LOG2E)
        if i == j:
            prob = jnp.where(key_id <= query_id, prob, 0.0)
        dprob = dot(heads_v[h, at_tile(j), :], upstream, nt)
        if want_q:
            dscore = prob * (dprob - delta)
            big = dscore.astype(jnp.bfloat16)
            rest = (dscore - big.astype(jnp.float32)).astype(jnp.bfloat16)
            turned = keys_t[:, at_tile(j)]
            grad = dot(turned, big, nn) + dot(turned, rest, nn)
            grad_t[...] = grad if fresh_q else grad_t[...] + grad
        if want_k:
            prob_k = prob * jnp.exp(lse - lse_w) if want_q else prob
            dscore_k = (prob_k * (dprob - wire(delta))).astype(jnp.bfloat16)
            grad_v = dot(prob_k.astype(jnp.bfloat16), upstream, nn)
            grad_k = dot(dscore_k, query, nn)
            acc_v[j % 2] = grad_v if fresh_k else acc_v[j % 2] + grad_v
            acc_k[j % 2] = grad_k if fresh_k else acc_k[j % 2] + grad_k

    results = ((res_q, gq_out), (res_k, gk_out), (res_v, gv_out))

    def give(a, h):
        src, dst = results[a]
        at = chunk(core * count + h, width)
        pltpu.make_async_copy(
            src.at[h, chunk(core, rows), :], dst.at[:, at], own_out.at[a]
        ).start()
        remote(
            src.at[h, chunk(other, rows), :],
            dst.at[:, at],
            send_out.at[a],
            recv_out.at[a],
            partner,
        ).start()

    def lse_copy(h, chip):
        if chip == 1:
            return remote(
                lse_mine.at[h], lse_in.at[h], send_l.at[h, 0], recv_l.at[h], 2 * chip + core
            )
        return remote(
            lse_mine.at[h, 1], lse_in.at[h, 1], send_l.at[h, 1], recv_l.at[h], 2 * chip + core
        )

    def edge_copy(h):
        return remote(
            edge_mine.at[h], edge_in.at[h], send_e.at[h], recv_e.at[h], 2 * 2 + core
        )

    def part_copy(h, chip):
        if chip == 0:
            return remote(
                part_mine.at[h], part_in.at[h], send_p.at[h], recv_p.at[h], 2 * chip + core
            )
        return remote(
            part_mine.at[h, 0], part_in.at[h, 0], send_p.at[h], recv_p.at[h], 2 * chip + core
        )

    def spread(row):
        return jnp.broadcast_to(row, (8, tile))

    def later_sums(h):
        for a, chip in ((0, 2), (1, 2), (1, 0), (1, 1), (0, 3)):
            arrive(a, chip, h)
        edge_copy(h).wait_recv()
        lse_mine[h, 0] = spread(log_sums(h, 2, (0, 1, 2)))
        near = log_sums(h, 3, (0, 1, 2))
        far = edge_in[h][0:1, :]
        top = jnp.maximum(near, far)
        lse_mine[h, 1] = spread(top + jnp.log(jnp.exp(near - top) + jnp.exp(far - top)))
        lse_copy(h, 1).start()
        lse_copy(h, 3).start()

    def head_first(h):
        for a in range(4):
            arrive(a, 0, h)
        turn_keys(h, 0)
        pair(h, 0, 0, log_sums(h, 0, (0,)), True, True, True, True)
        res_q[h] = (grad_t[...] * scale).T.astype(jnp.bfloat16)
        give(0, h)
        part_copy(h, 0).wait_recv()
        res_k[h] = ((acc_k[0] + part_in[h, 0].astype(jnp.float32)) * scale).astype(jnp.bfloat16)
        res_v[h] = (acc_v[0] + part_in[h, 1].astype(jnp.float32)).astype(jnp.bfloat16)
        give(1, h)
        give(2, h)

    def head_second(h):
        for a in range(4):
            arrive(a, 1, h)
        arrive(1, 0, h)
        lse = log_sums(h, 1, (0, 1))
        turn_keys(h, 0)
        turn_keys(h, 1)
        arrive(2, 0, h)
        pair(h, 1, 0, lse, True, True, True, True)
        pair(h, 1, 1, lse, True, True, False, True)
        res_q[h] = (grad_t[...] * scale).T.astype(jnp.bfloat16)
        give(0, h)
        lse_copy(h, 1).wait_recv()
        for i in (2, 3):
            arrive(0, i, h)
            arrive(3, i, h)
            for j in (0, 1):
                pair(h, i, j, lse_in[h, i - 2][0:1, :], False, True)
        part_mine[h, 0] = acc_k[0].astype(jnp.bfloat16)
        part_mine[h, 1] = acc_v[0].astype(jnp.bfloat16)
        part_copy(h, 0).start()
        res_k[h] = (acc_k[1] * scale).astype(jnp.bfloat16)
        res_v[h] = acc_v[1].astype(jnp.bfloat16)
        give(1, h)
        give(2, h)

    def head_third(h):
        @pl.when(h < count - 1)
        def _():
            later_sums(h + 1)

        for j in range(3):
            turn_keys(h, j)
        for a, chip in ((2, 2), (3, 2), (2, 0), (2, 1), (3, 3)):
            arrive(a, chip, h)
        lse = lse_mine[h, 1][0:1, :]
        pair(h, 3, 0, lse, True, False, True)
        pair(h, 3, 1, lse, True, False)
        pair(h, 3, 2, lse, True, True, False, True)
        part_mine[h, 0] = grad_t[...].T.astype(jnp.bfloat16)
        part_copy(h, 3).start()
        lse = lse_mine[h, 0][0:1, :]
        pair(h, 2, 0, lse, True, False, True)
        pair(h, 2, 1, lse, True, False)
        pair(h, 2, 2, lse, True, True)
        res_q[h] = (grad_t[...] * scale).T.astype(jnp.bfloat16)
        res_k[h] = (acc_k[0] * scale).astype(jnp.bfloat16)
        res_v[h] = acc_v[0].astype(jnp.bfloat16)
        for a in range(3):
            give(a, h)

    def head_last(h):
        for a in (2, 3):
            arrive(a, 3, h)
        lse_copy(h, 3).wait_recv()
        turn_keys(h, 3)
        pair(h, 3, 3, lse_in[h, 1][0:1, :], True, True, True, True)
        res_k[h] = (acc_k[1] * scale).astype(jnp.bfloat16)
        res_v[h] = acc_v[1].astype(jnp.bfloat16)
        give(1, h)
        give(2, h)
        part_copy(h, 3).wait_recv()
        total = grad_t[...].T + part_in[h, 0].astype(jnp.float32)
        res_q[h] = (total * scale).astype(jnp.bfloat16)
        give(0, h)

    for chip in range(CHIPS):

        @pl.when(z == chip)
        def _():
            delta_wait(chip)

    @pl.when(z == 3)
    def _():
        def edge(h, carry):
            arrive(0, 3, h)
            arrive(1, 3, h)
            edge_mine[h] = spread(log_sums(h, 3, (3,)))
            edge_copy(h).start()
            return carry

        lax.fori_loop(0, count, edge, 0)

    loads[4].wait()
    loads[5].wait()
    terms[...] = jnp.zeros_like(terms)
    both = jnp.concatenate([filters[...]] * (LANES // filters.shape[0]), axis=0)
    taps[...] = both.T

    def conv_own(t, carry):
        at = pl.ds(pl.multiple_of(t * LANES, LANES), LANES)
        mixed = fk[:, at].astype(jnp.float32) * fv[:, at].astype(jnp.float32)
        for a in range(span // 8):
            size = rows - 8 * a
            part = None
            for b in range(8):
                tap = 8 * a + b
                x = dz_all[t, tap : tap + size, :]
                term = x * taps[tap : tap + 1, :]
                part = term if part is None else part + term
                prod = (x * mixed[0:size]).reshape(size // 8, 8, LANES)
                terms[tap] = terms[tap] + jnp.sum(prod, axis=0)
            if a == 0:
                dw_all[t] = part
            else:
                dw_all[t, 0:size, :] = dw_all[t, 0:size, :] + part
        return carry

    lax.fori_loop(0, tiles, conv_own, 0)

    @pl.when(z == 1)
    def _():
        delta_wait(2)
        delta_wait(3)

    @pl.when(z == 2)
    def _():
        delta_wait(3)
        later_sums(0)

    def rim_part():
        @pl.when(me < n - 1)
        def _():
            rim_copy().wait_recv()
            for t in range(tiles):
                at = slice(t * LANES, (t + 1) * LANES)
                rim_all[t, 0:8, :] = jnp.zeros((8, LANES), jnp.float32)
                rim_all[t, 8 : rows + 8, :] = dz_rim[:, at].astype(jnp.float32)

        @pl.when(me == n - 1)
        def _():
            for t in range(tiles):
                rim_all[t, 0 : rows + 8, :] = jnp.zeros((rows + 8, LANES), jnp.float32)

        def conv_rim(t, carry):
            at = pl.ds(pl.multiple_of(t * LANES, LANES), LANES)
            left = fk[:, at].astype(jnp.float32)
            right = fv[:, at].astype(jnp.float32)
            mixed = left * right
            for a in range(span // 8):
                size = 8 * (a + 1)
                part = None
                for b in range(8):
                    tap = 8 * a + b
                    x = rim_all[t, b : b + size, :]
                    term = x * taps[tap : tap + 1, :]
                    part = term if part is None else part + term
                    prod = (x * mixed[rows - size : rows]).reshape(size // 8, 8, LANES)
                    terms[tap] = terms[tap] + jnp.sum(prod, axis=0)
                dw_all[t, rows - size : rows, :] = dw_all[t, rows - size : rows, :] + part
            acc = dw_all[t]
            gfk_out[:, at] = (acc * right).astype(jnp.bfloat16)
            gfv_out[:, at] = (acc * left).astype(jnp.bfloat16)
            return carry

        lax.fori_loop(0, tiles, conv_rim, 0)
    share = gf_out.shape[0] // n

    def slab(i):
        return chunk(i, share)

    def seq_copy(d):
        peer = lax.rem(me + d, n)
        return remote(
            partial_mine.at[slab(peer), :], partial_in.at[me], send_rs.at[d], recv_rs.at[d], peer
        )

    def tp_copy(d):
        return pltpu.make_async_remote_copy(
            src_ref=across.at[lane],
            dst_ref=across.at[lane],
            send_sem=send_tp.at[d],
            recv_sem=recv_tp.at[d],
            device_id={"tp": lax.rem(lane + d, tp)},
            device_id_type=MESH,
        )

    def all_copy(d):
        at = gf_out.at[slab(me), :]
        return remote(at, at, send_ag.at[d], recv_ag.at[d], lax.rem(me + d, n))

    def sum_here():
        per_lane = jnp.sum(terms[...], axis=1)
        groups = gf_out.shape[0]
        folded = per_lane
        for g in range(1, LANES // groups):
            folded = folded + pltpu.roll(per_lane, g * groups, 1)
        partial_mine[...] = folded.T[0:groups, :]
        partial_in[me] = partial_mine[slab(me), :]
        for d in range(1, n):
            seq_copy(d).start()

    def sum_seq():
        for d in range(1, n):
            seq_copy(d).wait_recv()
        total = partial_in[0]
        for i in range(1, n):
            total = total + partial_in[i]
        across[lane] = total
        for d in range(1, tp):
            tp_copy(d).start()

    def sum_tp():
        for d in range(1, tp):
            tp_copy(d).wait_recv()
        total = across[0]
        for i in range(1, tp):
            total = total + across[i]
        count_all = rows * n * channels * tp / gf_out.shape[0]
        gf_out[slab(me), :] = total * (1.0 / count_all**0.5)
        for d in range(1, n):
            all_copy(d).start()

    def per_head(h, carry):
        @pl.when(h == count // 2)
        def _():
            rim_part()
            sum_here()

        @pl.when(h == count - 1)
        def _():
            sum_seq()

        for chip, work in enumerate((head_first, head_second, head_third, head_last)):

            @pl.when(z == chip)
            def _():
                work(h)

        return carry

    lax.fori_loop(0, count, per_head, 0)
    sum_tp()

    @pl.when(me > 0)
    def _():
        rim_copy().wait_send()

    for a in range(4):
        moved(a, z, other).wait_send()
    delta_copy(z, other).wait_send()
    for chip in range(CHIPS):

        @pl.when(z == chip)
        def _():
            for a, to in CROSS[chip]:
                for side in range(2):
                    moved(a, to, side).wait_send()
            for to in DELTAS.get(chip, ()):
                for side in range(2):
                    delta_copy(to, side).wait_send()
            for h in range(count):
                if chip == 1:
                    part_copy(h, 0).wait_send()
                if chip == 2:
                    part_copy(h, 3).wait_send()
                    lse_copy(h, 1).wait_send()
                    lse_copy(h, 3).wait_send()
                if chip == 3:
                    edge_copy(h).wait_send()

    for a in range(3):
        dst = results[a][1]
        mine = dst.at[:, chunk(core, half)]
        theirs = dst.at[:, chunk(other, half)]
        pltpu.make_async_copy(mine, mine, own_out.at[a]).wait()
        remote(theirs, theirs, send_out.at[a], recv_out.at[a], partner).wait()
    for d in range(1, n):
        seq_copy(d).wait_send()
        all_copy(d).wait()
    for d in range(1, tp):
        tp_copy(d).wait_send()


def finish(
    gy_in,
    co_in,
    gq_in,
    gk_in,
    gv_in,
    gfk_in,
    gfv_in,
    gf_in,
    gq_out,
    gk_out,
    gv_out,
    gg_out,
    gfk_out,
    gfv_out,
    gf_out,
    gy,
    co,
    gg,
    gq,
    gk,
    gv,
    gfk,
    gfv,
    gf,
    sem_in,
    sem_out,
):
    sources = (gy_in, co_in, gq_in, gk_in, gv_in, gfk_in, gfv_in, gf_in)
    holds = (gy, co, gq, gk, gv, gfk, gfv, gf)
    taken = [
        pltpu.make_async_copy(src, dst, sem_in.at[i])
        for i, (src, dst) in enumerate(zip(sources, holds))
    ]
    for copy in taken:
        copy.start()
    given = []

    def give(src, dst):
        copy = pltpu.make_async_copy(src, dst, sem_out.at[len(given)])
        copy.start()
        given.append(copy)

    outs = (gq_out, gk_out, gv_out, gfk_out, gfv_out, gf_out)
    taken[0].wait()
    taken[1].wait()
    gg[...] = (gy[...].astype(jnp.float32) * co[...].astype(jnp.float32)).astype(jnp.bfloat16)
    give(gg, gg_out)
    for i, dst in enumerate(outs):
        taken[2 + i].wait()
        give(holds[2 + i], dst)
    for copy in given:
        copy.wait()


def local_heads(
    n,
    tp,
    q_heads,
    k_heads,
    v_heads,
    grad_attn,
    attn_out,
    gate_q,
    feat_k,
    feat_v,
    conv_out,
    grad_y,
    filters,
):
    rows, wide = q_heads.shape
    width = LANES
    count = wide // width // 2
    tile = 2 * rows
    channels = gate_q.shape[1]
    groups, span = filters.shape
    share = groups // n
    tiles = channels // LANES
    bf16, f32 = (jnp.bfloat16, jnp.float32)
    anywhere = pl.BlockSpec(memory_space=pl.ANY)
    inside = pl.BlockSpec(memory_space=pltpu.VMEM)
    dma = pltpu.SemaphoreType.DMA
    vmem = pltpu.VMEM
    small = [jax.ShapeDtypeStruct((rows, wide), bf16)] * 3
    large = [jax.ShapeDtypeStruct((rows, channels), bf16)] * 2
    last = [jax.ShapeDtypeStruct((groups, span), f32)]
    parts = pl.pallas_call(
        functools.partial(kernel, n, tp),
        out_shape=small + large + last,
        in_specs=[anywhere] * 9 + [inside],
        out_specs=[anywhere] * 3 + [inside] * 3,
        scratch_shapes=(
            [vmem((count, n * rows, width), bf16)] * 4
            + [
                vmem((width, n * rows), bf16),
                vmem((2, count, 8, rows), f32),
                vmem((n, count, 8, rows), f32),
                vmem((count, 2, 8, tile), f32),
                vmem((count, 2, 8, tile), f32),
                vmem((count, 8, tile), f32),
                vmem((count, 8, tile), f32),
                vmem((count, 2, tile, width), bf16),
                vmem((count, 2, tile, width), bf16),
            ]
            + [vmem((rows, wide), bf16)] * 2
            + [vmem((rows, channels), bf16)] * 6
            + [
                vmem((tiles, rows + 8, LANES), f32),
                vmem((tiles, rows + 16, LANES), f32),
                vmem((tiles, rows, LANES), f32),
                vmem((span, LANES), f32),
                vmem((span, 8, LANES), f32),
                vmem((groups, span), f32),
                vmem((n, share, span), f32),
                vmem((tp, share, span), f32),
                vmem((n * rows, tile), f32),
                vmem((width, tile), f32),
            ]
            + [vmem((2, tile, width), f32)] * 2
            + [vmem((count, tile, width), bf16)] * 3
            + [
                dma((6,)),
                dma((4, CHIPS, 2)),
                dma((4, CHIPS, count)),
                dma((CHIPS, 2)),
                dma((n,)),
                dma((count, 2)),
                dma((count,)),
                dma((count,)),
                dma((count,)),
                dma((count,)),
                dma((count,)),
                dma,
                dma,
                dma((3,)),
                dma((3,)),
                dma((3,)),
                dma((n,)),
                dma((n,)),
                dma((tp,)),
                dma((tp,)),
                dma((n,)),
                dma((n,)),
            ]
        ),
        compiler_params=pltpu.CompilerParams(
            collective_id=0, has_side_effects=True, vmem_limit_bytes=67043328
        ),
    )(q_heads, k_heads, v_heads, grad_attn, attn_out, gate_q, feat_k, feat_v, grad_y, filters)
    return pl.pallas_call(
        finish,
        out_shape=small + large[:1] + large + last,
        in_specs=[anywhere] * 8,
        out_specs=[anywhere] * 7,
        scratch_shapes=(
            [vmem((rows, channels), bf16)] * 3
            + [vmem((rows, wide), bf16)] * 3
            + [vmem((rows, channels), bf16)] * 2
            + [vmem((groups, span), f32), dma((8,)), dma((7,))]
        ),
    )(grad_y, conv_out, *parts)


def local(*args):
    n, tp = (lax.axis_size("seq"), lax.axis_size("tp"))
    rows, wide = args[0].shape
    groups, span = args[10].shape
    fits = (
        HEADS // tp == n
        and n == 2 * CHIPS
        and tp > 1
        and rows == LANES
        and wide == n * LANES
        and span <= rows
        and span == LANES
        and LANES % groups == 0
        and groups % (8 * n) == 0
    )
    if fits:
        return tuple(local_heads(n, tp, *args))
    return local_ring(*args)


def solution(mesh):
    in_specs = (
        P("seq", "tp"),
        P("seq", "tp"),
        P("seq", "tp"),
        P("seq", "tp"),
        P("seq", "tp"),
        P("seq", "tp"),
        P("seq", "tp"),
        P("seq", "tp"),
        P("seq", "tp"),
        P("seq", "tp"),
        P(),
    )
    out_specs = (
        P("seq", "tp"),
        P("seq", "tp"),
        P("seq", "tp"),
        P("seq", "tp"),
        P("seq", "tp"),
        P("seq", "tp"),
        P(),
    )
    return jax.shard_map(local, mesh=mesh, in_specs=in_specs, out_specs=out_specs, check_vma=False)
```

```python
import functools

import jax
import jax.numpy as jnp
from jax import lax
from jax.experimental import pallas as pl
from jax.experimental.pallas import tpu as pltpu
from jax.sharding import PartitionSpec as P

HEADS = 32


def from_behind(value, axis, steps):
    count = lax.axis_size(axis)
    leading, last = (max(0, -steps), min(count, count - steps))
    return lax.ppermute(value, axis, [(source, source + steps) for source in range(leading, last)])


def wire_parts(x):
    high = x.astype(jnp.bfloat16)
    back = lax.optimization_barrier(high).astype(jnp.float32)
    low = (x - back).astype(jnp.bfloat16)
    return (high, low)


def local_ring(
    q_heads,
    k_heads,
    v_heads,
    grad_attn,
    attn_out,
    gate_q,
    feat_k,
    feat_v,
    conv_out,
    grad_y,
    filters,
):
    rows = q_heads.shape[0]
    heads_here = HEADS // lax.axis_size("tp")
    width = q_heads.shape[1] // heads_here
    scale = 1.0 / width**0.5
    shards = lax.axis_size("seq")
    place = lax.axis_index("seq")
    queries = q_heads.reshape(rows, heads_here, width)
    upstream = grad_attn.reshape(rows, heads_here, width)
    keys_here = k_heads.reshape(rows, heads_here, width)
    values_here = v_heads.reshape(rows, heads_here, width)
    delta = jnp.sum(
        upstream.astype(jnp.float32)
        * attn_out.reshape(rows, heads_here, width).astype(jnp.float32),
        axis=2,
    )
    delta_heads = delta.T
    diagonal = jnp.arange(rows)[:, None] >= jnp.arange(rows)[None, :]

    def query_tile(state, key_piece, value_piece, live):
        top, total, acc = state
        count = key_piece.shape[0]
        key_block = key_piece.reshape(count, heads_here, width)
        value_block = value_piece.reshape(count, heads_here, width)
        scores = (
            jnp.einsum("qhd,khd->hqk", queries, key_block, preferred_element_type=jnp.float32)
            * scale
        )
        top_new = jnp.maximum(top, jnp.max(jnp.where(live[None], scores, -1e30), axis=2))
        weights = jnp.where(live[None], jnp.exp(scores - top_new[:, :, None]), 0.0)
        decay = jnp.exp(top - top_new)
        dprob = jnp.einsum(
            "qhd,khd->hqk", upstream, value_block, preferred_element_type=jnp.float32
        )
        term = jnp.einsum(
            "hqk,khd->qhd",
            weights * (dprob - delta_heads[:, :, None]),
            key_block.astype(jnp.float32),
            precision=lax.Precision.HIGHEST,
        )
        return (top_new, total * decay + jnp.sum(weights, axis=2), acc * decay.T[:, :, None] + term)

    zero_rows = jnp.zeros((rows, heads_here, width), jnp.float32)
    state = (
        jnp.full((heads_here, rows), -1e30, jnp.float32),
        jnp.zeros((heads_here, rows), jnp.float32),
        zero_rows,
    )
    state = query_tile(state, k_heads, v_heads, diagonal)

    def relay_keys(back, carry):
        inner, moving = carry
        moving = from_behind((moving[0], moving[1]), "seq", 1)
        valid = place >= back
        live = jnp.broadcast_to(valid, (rows, rows))
        inner = query_tile(inner, moving[0], moving[1], live)
        return (inner, moving)

    state, moved = lax.fori_loop(1, shards, relay_keys, (state, (k_heads, v_heads)))
    top, total, acc = state
    lse = (top + jnp.log(total)).T
    grad_query = acc * (1.0 / total).T[:, :, None] * scale
    lse_high, lse_low = wire_parts(lse)
    delta_high, delta_low = wire_parts(delta)
    stats = jnp.stack([lse_high, lse_low, delta_high, delta_low], axis=1)

    def key_tile(inner, query_piece, upstream_piece, stat_piece, live):
        key_grad, value_grad = inner
        count = query_piece.shape[0]
        query_block = query_piece.reshape(count, heads_here, width)
        upstream_block = upstream_piece.reshape(count, heads_here, width)
        lse_w = stat_piece[:, 0].astype(jnp.float32) + stat_piece[:, 1].astype(jnp.float32)
        delta_w = stat_piece[:, 2].astype(jnp.float32) + stat_piece[:, 3].astype(jnp.float32)
        scores = (
            jnp.einsum("qhd,khd->hqk", query_block, keys_here, preferred_element_type=jnp.float32)
            * scale
        )
        probs = jnp.where(live[None], jnp.exp(scores - lse_w.T[:, :, None]), 0.0)
        dprob = jnp.einsum(
            "qhd,khd->hqk", upstream_block, values_here, preferred_element_type=jnp.float32
        )
        dscore = probs * (dprob - delta_w.T[:, :, None])
        value_grad = value_grad + jnp.einsum(
            "hqk,qhd->khd",
            probs.astype(jnp.bfloat16),
            upstream_block,
            preferred_element_type=jnp.float32,
        )
        key_grad = key_grad + jnp.einsum(
            "hqk,qhd->khd",
            dscore.astype(jnp.bfloat16),
            query_block,
            preferred_element_type=jnp.float32,
        )
        return (key_grad, value_grad)

    grads = (zero_rows, zero_rows)
    grads = key_tile(grads, q_heads, grad_attn, stats, diagonal)

    def relay_queries(back, carry):
        inner, moving = carry
        moving = from_behind((moving[0], moving[1], moving[2]), "seq", -1)
        valid = place + back <= shards - 1
        live = jnp.broadcast_to(valid, (rows, rows))
        inner = key_tile(inner, moving[0], moving[1], moving[2], live)
        return (inner, moving)

    grads, moved = lax.fori_loop(1, shards, relay_queries, (grads, (q_heads, grad_attn, stats)))
    key_grad, value_grad = grads
    grad_q = grad_query.astype(jnp.bfloat16).reshape(rows, heads_here * width)
    grad_k = (key_grad * scale).astype(jnp.bfloat16).reshape(rows, heads_here * width)
    grad_v = value_grad.astype(jnp.bfloat16).reshape(rows, heads_here * width)
    span_taps = filters.shape[1]
    groups = filters.shape[0]
    channels = gate_q.shape[1]
    dz = (grad_y.astype(jnp.float32) * gate_q.astype(jnp.float32)).astype(jnp.bfloat16)
    rim = from_behind(dz[: span_taps - 1], "seq", -1)
    grad_gate = (grad_y.astype(jnp.float32) * conv_out.astype(jnp.float32)).astype(jnp.bfloat16)
    padded = jnp.concatenate([dz, rim], axis=0).astype(jnp.float32)
    taps = jnp.tile(filters.T, (1, channels // groups))
    mixed = feat_k.astype(jnp.float32) * feat_v.astype(jnp.float32)
    numbers = ("NWC", "WIO", "NWC")
    dw = lax.conv_general_dilated(
        padded[None],
        taps[:, None, :],
        (1,),
        "VALID",
        dimension_numbers=numbers,
        feature_group_count=channels,
        precision=lax.Precision.HIGHEST,
    )[0]
    local_terms = lax.conv_general_dilated(
        padded[None],
        mixed[:, None, :],
        (1,),
        "VALID",
        dimension_numbers=numbers,
        feature_group_count=channels,
        precision=lax.Precision.HIGHEST,
    )[0]
    grad_feat_k = (dw * feat_v.astype(jnp.float32)).astype(jnp.bfloat16)
    grad_feat_v = (dw * feat_k.astype(jnp.float32)).astype(jnp.bfloat16)
    local_terms = jnp.sum(local_terms.reshape(span_taps, channels // groups, groups), axis=1).T
    filter_total = lax.psum(local_terms, ("seq", "tp"))
    count_all = rows * shards * channels * lax.axis_size("tp") / groups
    grad_filters = filter_total * (1.0 / count_all**0.5)
    return (grad_q, grad_k, grad_v, grad_gate, grad_feat_k, grad_feat_v, grad_filters)


MESH = pl.DeviceIdType.MESH
LANES = 128
LOG2E = 1.4426950408889634
CHIPS = 4
CROSS = {0: ((1, 2), (1, 1), (2, 2), (2, 1)), 1: ((1, 2), (2, 2)), 2: ((0, 1), (3, 1)), 3: ((0, 2), (0, 1), (3, 2), (3, 1))}
DELTAS = {2: (1,), 3: (2, 1)}


def kernel(
    n,
    tp,
    q_in,
    k_in,
    v_in,
    do_in,
    ao_in,
    gate_in,
    fk_in,
    fv_in,
    gy_in,
    filters,
    gq_out,
    gk_out,
    gv_out,
    gfk_out,
    gfv_out,
    gf_out,
    heads_q,
    heads_k,
    heads_v,
    heads_do,
    keys_t,
    delta_mine,
    delta_all,
    lse_mine,
    lse_in,
    edge_mine,
    edge_in,
    part_mine,
    part_in,
    do_here,
    ao_here,
    gate,
    fk,
    fv,
    gy,
    dz_here,
    dz_rim,
    dz_all,
    rim_all,
    dw_all,
    taps,
    terms,
    partial_mine,
    partial_in,
    across,
    scores,
    grad_t,
    acc_k,
    acc_v,
    res_q,
    res_k,
    res_v,
    load_sem,
    send_x,
    recv_x,
    send_d,
    recv_d,
    send_l,
    recv_l,
    send_e,
    recv_e,
    send_p,
    recv_p,
    send_rim,
    recv_rim,
    send_out,
    recv_out,
    own_out,
    send_rs,
    recv_rs,
    send_tp,
    recv_tp,
    send_ag,
    recv_ag,
):
    me = lax.axis_index("seq")
    lane = lax.axis_index("tp")
    z = lax.div(me, 2)
    core = lax.rem(me, 2)
    other = 1 - core
    partner = 2 * z + other
    rows, width = q_in.shape[0], LANES
    count = q_in.shape[1] // width // 2
    half = count * width
    tile = 2 * rows
    channels = gy_in.shape[1]
    span = filters.shape[1]
    scale = 1.0 / width**0.5

    def chunk(i, size):
        return pl.ds(pl.multiple_of(i * size, size), size)

    def remote(src, dst, send, recv, device):
        return pltpu.make_async_remote_copy(
            src_ref=src,
            dst_ref=dst,
            send_sem=send,
            recv_sem=recv,
            device_id={"seq": device},
            device_id_type=MESH,
        )

    loads = [
        pltpu.make_async_copy(src, dst, load_sem.at[i])
        for i, (src, dst) in enumerate(
            (
                (do_in, do_here),
                (ao_in, ao_here),
                (gy_in, gy),
                (gate_in, gate),
                (fk_in, fk),
                (fv_in, fv),
            )
        )
    ]
    for load in loads:
        load.start()

    barrier = pltpu.get_barrier_semaphore()
    for d in range(1, n):
        pl.semaphore_signal(
            barrier, inc=1, device_id={"seq": lax.rem(me + d, n)}, device_id_type=MESH
        )
    for d in range(1, tp):
        pl.semaphore_signal(
            barrier, inc=1, device_id={"tp": lax.rem(lane + d, tp)}, device_id_type=MESH
        )
    pl.semaphore_wait(barrier, n - 1 + tp - 1)

    ins = (q_in, k_in, v_in, do_in)
    heads = (heads_q, heads_k, heads_v, heads_do)

    def move(a, h, chip, to):
        return remote(
            ins[a].at[:, chunk(to * count + h, width)],
            heads[a].at[h, chunk(me, rows), :],
            send_x.at[a, chip, to],
            recv_x.at[a, z, h],
            2 * chip + to,
        )

    def moved(a, chip, to):
        return remote(
            ins[a].at[:, chunk(to, half)],
            ins[a].at[:, chunk(to, half)],
            send_x.at[a, chip, to],
            recv_x.at[a, chip, 0],
            2 * chip + to,
        )

    def own(a, h):
        return pltpu.make_async_copy(
            ins[a].at[:, chunk(core * count + h, width)],
            heads[a].at[h, chunk(me, rows), :],
            recv_x.at[a, z, h],
        )

    def arrive(a, chip, h):
        at = heads[a].at[h, chunk(chip, tile), :]
        remote(at, at, send_x.at[a, 0, 0], recv_x.at[a, chip, h], partner).wait_recv()

    def exchange(h):
        for a in (0, 1, 3, 2):
            own(a, h).start()
            move(a, h, z, other).start()

    def outward(h):
        for chip in range(CHIPS):

            @pl.when(z == chip)
            def _():
                for a, to in CROSS[chip]:
                    for side in range(2):
                        move(a, h, to, side).start()

    def rim_copy():
        return remote(dz_here, dz_rim, send_rim, recv_rim, lax.rem(me + n - 1, n))

    def delta_copy(chip, to):
        return remote(
            delta_mine.at[to],
            delta_all.at[me],
            send_d.at[chip, to],
            recv_d.at[me],
            2 * chip + to,
        )

    def delta_wait(chip):
        for side in range(2):
            b = 2 * chip + side
            at = delta_all.at[b]

            @pl.when(b != me)
            def _():
                remote(at, at, send_d.at[0, 0], recv_d.at[b], partner).wait_recv()

    for h in range(count):
        exchange(h)
    outward(0)

    loads[0].wait()
    loads[1].wait()
    for h in range(2 * count):
        at = slice(h * width, (h + 1) * width)
        prod = do_here[:, at].astype(jnp.float32) * ao_here[:, at].astype(jnp.float32)
        line = jnp.sum(prod.T, axis=0, keepdims=True)
        delta_mine[h // count, h % count] = jnp.broadcast_to(line, (8, rows))
    delta_all[me] = delta_mine[core]
    delta_copy(z, other).start()
    for chip, targets in DELTAS.items():

        @pl.when(z == chip)
        def _():
            for to in targets:
                for side in range(2):
                    delta_copy(to, side).start()

    key_id = lax.broadcasted_iota(jnp.int32, (tile, tile), 0)
    query_id = lax.broadcasted_iota(jnp.int32, (tile, tile), 1)
    nt = (((1,), (1,)), ((), ()))
    nn = (((1,), (0,)), ((), ()))

    def dot(a, b, dims):
        return lax.dot_general(a, b, dims, preferred_element_type=jnp.float32)

    def at_tile(i):
        return slice(i * tile, (i + 1) * tile)

    def log_sums(h, i, keys):
        query = heads_q[h, at_tile(i), :]
        top = None
        for j in keys:
            raw = dot(heads_k[h, at_tile(j), :], query, nt)
            if j == i:
                raw = jnp.where(key_id <= query_id, raw, -1e30)
            scores[at_tile(j), :] = raw
            high = jnp.max(raw, axis=0, keepdims=True)
            top = high if top is None else jnp.maximum(top, high)
        total = jnp.zeros_like(top)
        for j in keys:
            weight = jnp.exp2((scores[at_tile(j), :] - top) * (scale * LOG2E))
            total = total + jnp.sum(weight, axis=0, keepdims=True)
        return top * scale + jnp.log(total)

    def wire(x):
        high = x.astype(jnp.bfloat16).astype(jnp.float32)
        return high + (x - high).astype(jnp.bfloat16).astype(jnp.float32)

    def delta_row(h, i):
        return jnp.concatenate(
            [delta_all[2 * i, h][0:1, :], delta_all[2 * i + 1, h][0:1, :]], axis=1
        )

    def turn_keys(h, j):
        keys_t[:, at_tile(j)] = heads_k[h, at_tile(j), :].T

    def pair(h, i, j, lse, want_q, want_k, fresh_q=False, fresh_k=False):
        query = heads_q[h, at_tile(i), :]
        upstream = heads_do[h, at_tile(i), :]
        delta = delta_row(h, i)
        lse_w = wire(lse)
        base = lse if want_q else lse_w
        raw = dot(heads_k[h, at_tile(j), :], query, nt)
        prob = jnp.exp2(raw * (scale * LOG2E) - base * LOG2E)
        if i == j:
            prob = jnp.where(key_id <= query_id, prob, 0.0)
        dprob = dot(heads_v[h, at_tile(j), :], upstream, nt)
        if want_q:
            dscore = prob * (dprob - delta)
            big = dscore.astype(jnp.bfloat16)
            rest = (dscore - big.astype(jnp.float32)).astype(jnp.bfloat16)
            turned = keys_t[:, at_tile(j)]
            grad = dot(turned, big, nn) + dot(turned, rest, nn)
            grad_t[...] = grad if fresh_q else grad_t[...] + grad
        if want_k:
            prob_k = prob * jnp.exp(lse - lse_w) if want_q else prob
            dscore_k = (prob_k * (dprob - wire(delta))).astype(jnp.bfloat16)
            grad_v = dot(prob_k.astype(jnp.bfloat16), upstream, nn)
            grad_k = dot(dscore_k, query, nn)
            acc_v[j % 2] = grad_v if fresh_k else acc_v[j % 2] + grad_v
            acc_k[j % 2] = grad_k if fresh_k else acc_k[j % 2] + grad_k

    results = ((res_q, gq_out), (res_k, gk_out), (res_v, gv_out))

    def give(a, h):
        src, dst = results[a]
        at = chunk(core * count + h, width)
        pltpu.make_async_copy(
            src.at[h, chunk(core, rows), :], dst.at[:, at], own_out.at[a]
        ).start()
        remote(
            src.at[h, chunk(other, rows), :],
            dst.at[:, at],
            send_out.at[a],
            recv_out.at[a],
            partner,
        ).start()

    def lse_copy(h, chip):
        if chip == 1:
            return remote(
                lse_mine.at[h], lse_in.at[h], send_l.at[h, 0], recv_l.at[h], 2 * chip + core
            )
        return remote(
            lse_mine.at[h, 1], lse_in.at[h, 1], send_l.at[h, 1], recv_l.at[h], 2 * chip + core
        )

    def edge_copy(h):
        return remote(
            edge_mine.at[h], edge_in.at[h], send_e.at[h], recv_e.at[h], 2 * 2 + core
        )

    def part_copy(h, chip):
        if chip == 0:
            return remote(
                part_mine.at[h], part_in.at[h], send_p.at[h], recv_p.at[h], 2 * chip + core
            )
        return remote(
            part_mine.at[h, 0], part_in.at[h, 0], send_p.at[h], recv_p.at[h], 2 * chip + core
        )

    def spread(row):
        return jnp.broadcast_to(row, (8, tile))

    def later_sums(h):
        for a, chip in ((0, 2), (1, 2), (1, 0), (1, 1), (0, 3)):
            arrive(a, chip, h)
        edge_copy(h).wait_recv()
        lse_mine[h, 0] = spread(log_sums(h, 2, (0, 1, 2)))
        near = log_sums(h, 3, (0, 1, 2))
        far = edge_in[h][0:1, :]
        top = jnp.maximum(near, far)
        lse_mine[h, 1] = spread(top + jnp.log(jnp.exp(near - top) + jnp.exp(far - top)))
        lse_copy(h, 1).start()
        lse_copy(h, 3).start()

        @pl.when(h < count - 2)
        def _():
            outward(h + 2)

    def head_first(h):
        for a in range(4):
            arrive(a, 0, h)
        turn_keys(h, 0)
        pair(h, 0, 0, log_sums(h, 0, (0,)), True, True, True, True)
        res_q[h] = (grad_t[...] * scale).T.astype(jnp.bfloat16)
        give(0, h)
        part_copy(h, 0).wait_recv()
        res_k[h] = ((acc_k[0] + part_in[h, 0].astype(jnp.float32)) * scale).astype(jnp.bfloat16)
        res_v[h] = (acc_v[0] + part_in[h, 1].astype(jnp.float32)).astype(jnp.bfloat16)
        give(1, h)
        give(2, h)

    def head_second(h):
        for a in range(4):
            arrive(a, 1, h)
        arrive(1, 0, h)
        lse = log_sums(h, 1, (0, 1))
        turn_keys(h, 0)
        turn_keys(h, 1)
        arrive(2, 0, h)
        pair(h, 1, 0, lse, True, True, True, True)
        pair(h, 1, 1, lse, True, True, False, True)
        res_q[h] = (grad_t[...] * scale).T.astype(jnp.bfloat16)
        give(0, h)
        lse_copy(h, 1).wait_recv()
        for i in (2, 3):
            arrive(0, i, h)
            arrive(3, i, h)
            for j in (0, 1):
                pair(h, i, j, lse_in[h, i - 2][0:1, :], False, True)
        part_mine[h, 0] = acc_k[0].astype(jnp.bfloat16)
        part_mine[h, 1] = acc_v[0].astype(jnp.bfloat16)
        part_copy(h, 0).start()
        res_k[h] = (acc_k[1] * scale).astype(jnp.bfloat16)
        res_v[h] = acc_v[1].astype(jnp.bfloat16)
        give(1, h)
        give(2, h)

    def head_third(h):
        @pl.when(h < count - 1)
        def _():
            later_sums(h + 1)

        for j in range(3):
            turn_keys(h, j)
        for a, chip in ((2, 2), (3, 2), (2, 0), (2, 1), (3, 3)):
            arrive(a, chip, h)
        lse = lse_mine[h, 1][0:1, :]
        pair(h, 3, 0, lse, True, False, True)
        pair(h, 3, 1, lse, True, False)
        pair(h, 3, 2, lse, True, True, False, True)
        part_mine[h, 0] = grad_t[...].T.astype(jnp.bfloat16)
        part_copy(h, 3).start()
        lse = lse_mine[h, 0][0:1, :]
        pair(h, 2, 0, lse, True, False, True)
        pair(h, 2, 1, lse, True, False)
        pair(h, 2, 2, lse, True, True)
        res_q[h] = (grad_t[...] * scale).T.astype(jnp.bfloat16)
        res_k[h] = (acc_k[0] * scale).astype(jnp.bfloat16)
        res_v[h] = acc_v[0].astype(jnp.bfloat16)
        for a in range(3):
            give(a, h)

    def head_last(h):
        for a in (2, 3):
            arrive(a, 3, h)
        lse_copy(h, 3).wait_recv()
        turn_keys(h, 3)
        pair(h, 3, 3, lse_in[h, 1][0:1, :], True, True, True, True)
        res_k[h] = (acc_k[1] * scale).astype(jnp.bfloat16)
        res_v[h] = acc_v[1].astype(jnp.bfloat16)
        give(1, h)
        give(2, h)
        part_copy(h, 3).wait_recv()
        total = grad_t[...].T + part_in[h, 0].astype(jnp.float32)
        res_q[h] = (total * scale).astype(jnp.bfloat16)
        give(0, h)

    @pl.when(z == 3)
    def _():
        def edge(h, carry):
            arrive(0, 3, h)
            arrive(1, 3, h)
            edge_mine[h] = spread(log_sums(h, 3, (3,)))
            edge_copy(h).start()
            return carry

        lax.fori_loop(0, count, edge, 0)

    loads[2].wait()
    loads[3].wait()
    tiles = channels // LANES
    for t in range(tiles):
        at = slice(t * LANES, (t + 1) * LANES)
        dz = (gy[:, at].astype(jnp.float32) * gate[:, at].astype(jnp.float32)).astype(jnp.bfloat16)
        dz_here[:, at] = dz
        dz_all[t, 0:rows, :] = dz.astype(jnp.float32)
        dz_all[t, rows : rows + 8, :] = jnp.zeros((8, LANES), jnp.float32)

    @pl.when(me > 0)
    def _():
        rim_copy().start()

    outward(1)

    @pl.when(z != 2)
    def _():
        outward(2)

    @pl.when(z < 2)
    def _():
        outward(count - 1)

    for chip in range(CHIPS):

        @pl.when(z == chip)
        def _():
            delta_wait(chip)

    loads[4].wait()
    loads[5].wait()
    terms[...] = jnp.zeros_like(terms)
    both = jnp.concatenate([filters[...]] * (LANES // filters.shape[0]), axis=0)
    taps[...] = both.T

    def conv_own(t, carry):
        at = pl.ds(pl.multiple_of(t * LANES, LANES), LANES)
        mixed = fk[:, at].astype(jnp.float32) * fv[:, at].astype(jnp.float32)
        for a in range(span // 8):
            size = rows - 8 * a
            part = None
            for b in range(8):
                tap = 8 * a + b
                x = dz_all[t, tap : tap + size, :]
                term = x * taps[tap : tap + 1, :]
                part = term if part is None else part + term
                prod = (x * mixed[0:size]).reshape(size // 8, 8, LANES)
                terms[tap] = terms[tap] + jnp.sum(prod, axis=0)
            if a == 0:
                dw_all[t] = part
            else:
                dw_all[t, 0:size, :] = dw_all[t, 0:size, :] + part
        return carry

    lax.fori_loop(0, tiles, conv_own, 0)

    @pl.when(z == 1)
    def _():
        delta_wait(2)
        delta_wait(3)

    @pl.when(z == 2)
    def _():
        delta_wait(3)
        later_sums(0)

    def rim_part():
        @pl.when(me < n - 1)
        def _():
            rim_copy().wait_recv()
            for t in range(tiles):
                at = slice(t * LANES, (t + 1) * LANES)
                rim_all[t, 0:8, :] = jnp.zeros((8, LANES), jnp.float32)
                rim_all[t, 8 : rows + 8, :] = dz_rim[:, at].astype(jnp.float32)

        @pl.when(me == n - 1)
        def _():
            for t in range(tiles):
                rim_all[t, 0 : rows + 8, :] = jnp.zeros((rows + 8, LANES), jnp.float32)

        def conv_rim(t, carry):
            at = pl.ds(pl.multiple_of(t * LANES, LANES), LANES)
            left = fk[:, at].astype(jnp.float32)
            right = fv[:, at].astype(jnp.float32)
            mixed = left * right
            for a in range(span // 8):
                size = 8 * (a + 1)
                part = None
                for b in range(8):
                    tap = 8 * a + b
                    x = rim_all[t, b : b + size, :]
                    term = x * taps[tap : tap + 1, :]
                    part = term if part is None else part + term
                    prod = (x * mixed[rows - size : rows]).reshape(size // 8, 8, LANES)
                    terms[tap] = terms[tap] + jnp.sum(prod, axis=0)
                dw_all[t, rows - size : rows, :] = dw_all[t, rows - size : rows, :] + part
            acc = dw_all[t]
            gfk_out[:, at] = (acc * right).astype(jnp.bfloat16)
            gfv_out[:, at] = (acc * left).astype(jnp.bfloat16)
            return carry

        lax.fori_loop(0, tiles, conv_rim, 0)
    share = gf_out.shape[0] // n

    def slab(i):
        return chunk(i, share)

    def seq_copy(d):
        peer = lax.rem(me + d, n)
        return remote(
            partial_mine.at[slab(peer), :], partial_in.at[me], send_rs.at[d], recv_rs.at[d], peer
        )

    def tp_copy(d):
        return pltpu.make_async_remote_copy(
            src_ref=across.at[lane],
            dst_ref=across.at[lane],
            send_sem=send_tp.at[d],
            recv_sem=recv_tp.at[d],
            device_id={"tp": lax.rem(lane + d, tp)},
            device_id_type=MESH,
        )

    def all_copy(d):
        at = gf_out.at[slab(me), :]
        return remote(at, at, send_ag.at[d], recv_ag.at[d], lax.rem(me + d, n))

    def sum_here():
        per_lane = jnp.sum(terms[...], axis=1)
        groups = gf_out.shape[0]
        folded = per_lane
        for g in range(1, LANES // groups):
            folded = folded + pltpu.roll(per_lane, g * groups, 1)
        partial_mine[...] = folded.T[0:groups, :]
        partial_in[me] = partial_mine[slab(me), :]
        for d in range(1, n):
            seq_copy(d).start()

    def sum_seq():
        for d in range(1, n):
            seq_copy(d).wait_recv()
        total = partial_in[0]
        for i in range(1, n):
            total = total + partial_in[i]
        across[lane] = total
        for d in range(1, tp):
            tp_copy(d).start()

    def sum_tp():
        for d in range(1, tp):
            tp_copy(d).wait_recv()
        total = across[0]
        for i in range(1, tp):
            total = total + across[i]
        count_all = rows * n * channels * tp / gf_out.shape[0]
        gf_out[slab(me), :] = total * (1.0 / count_all**0.5)
        for d in range(1, n):
            all_copy(d).start()

    def per_head(h, carry):
        @pl.when(h == z * (CHIPS - 1 - z))
        def _():
            rim_part()
            sum_here()

            @pl.when(z == 3)
            def _():
                outward(count - 1)

        @pl.when(h == count - 1)
        def _():
            sum_seq()

        for chip, work in enumerate((head_first, head_second, head_third, head_last)):

            @pl.when(z == chip)
            def _():
                work(h)

        return carry

    lax.fori_loop(0, count, per_head, 0)
    sum_tp()

    @pl.when(me > 0)
    def _():
        rim_copy().wait_send()

    for a in range(4):
        moved(a, z, other).wait_send()
    delta_copy(z, other).wait_send()
    for chip in range(CHIPS):

        @pl.when(z == chip)
        def _():
            for a, to in CROSS[chip]:
                for side in range(2):
                    moved(a, to, side).wait_send()
            for to in DELTAS.get(chip, ()):
                for side in range(2):
                    delta_copy(to, side).wait_send()
            for h in range(count):
                if chip == 1:
                    part_copy(h, 0).wait_send()
                if chip == 2:
                    part_copy(h, 3).wait_send()
                    lse_copy(h, 1).wait_send()
                    lse_copy(h, 3).wait_send()
                if chip == 3:
                    edge_copy(h).wait_send()

    for a in range(3):
        dst = results[a][1]
        mine = dst.at[:, chunk(core, half)]
        theirs = dst.at[:, chunk(other, half)]
        pltpu.make_async_copy(mine, mine, own_out.at[a]).wait()
        remote(theirs, theirs, send_out.at[a], recv_out.at[a], partner).wait()
    for d in range(1, n):
        seq_copy(d).wait_send()
        all_copy(d).wait()
    for d in range(1, tp):
        tp_copy(d).wait_send()


def finish(
    gy_in,
    co_in,
    gq_in,
    gk_in,
    gv_in,
    gfk_in,
    gfv_in,
    gf_in,
    gq_out,
    gk_out,
    gv_out,
    gg_out,
    gfk_out,
    gfv_out,
    gf_out,
    gy,
    co,
    gg,
    gq,
    gk,
    gv,
    gfk,
    gfv,
    gf,
    sem_in,
    sem_out,
):
    sources = (gy_in, co_in, gq_in, gk_in, gv_in, gfk_in, gfv_in, gf_in)
    holds = (gy, co, gq, gk, gv, gfk, gfv, gf)
    taken = [
        pltpu.make_async_copy(src, dst, sem_in.at[i])
        for i, (src, dst) in enumerate(zip(sources, holds))
    ]
    for copy in taken:
        copy.start()
    given = []

    def give(src, dst):
        copy = pltpu.make_async_copy(src, dst, sem_out.at[len(given)])
        copy.start()
        given.append(copy)

    outs = (gq_out, gk_out, gv_out, gfk_out, gfv_out, gf_out)
    taken[0].wait()
    taken[1].wait()
    gg[...] = (gy[...].astype(jnp.float32) * co[...].astype(jnp.float32)).astype(jnp.bfloat16)
    give(gg, gg_out)
    for i, dst in enumerate(outs):
        taken[2 + i].wait()
        give(holds[2 + i], dst)
    for copy in given:
        copy.wait()


def local_heads(
    n,
    tp,
    q_heads,
    k_heads,
    v_heads,
    grad_attn,
    attn_out,
    gate_q,
    feat_k,
    feat_v,
    conv_out,
    grad_y,
    filters,
):
    rows, wide = q_heads.shape
    width = LANES
    count = wide // width // 2
    tile = 2 * rows
    channels = gate_q.shape[1]
    groups, span = filters.shape
    share = groups // n
    tiles = channels // LANES
    bf16, f32 = (jnp.bfloat16, jnp.float32)
    anywhere = pl.BlockSpec(memory_space=pl.ANY)
    inside = pl.BlockSpec(memory_space=pltpu.VMEM)
    dma = pltpu.SemaphoreType.DMA
    vmem = pltpu.VMEM
    small = [jax.ShapeDtypeStruct((rows, wide), bf16)] * 3
    large = [jax.ShapeDtypeStruct((rows, channels), bf16)] * 2
    last = [jax.ShapeDtypeStruct((groups, span), f32)]
    parts = pl.pallas_call(
        functools.partial(kernel, n, tp),
        out_shape=small + large + last,
        in_specs=[anywhere] * 9 + [inside],
        out_specs=[anywhere] * 3 + [inside] * 3,
        scratch_shapes=(
            [vmem((count, n * rows, width), bf16)] * 4
            + [
                vmem((width, n * rows), bf16),
                vmem((2, count, 8, rows), f32),
                vmem((n, count, 8, rows), f32),
                vmem((count, 2, 8, tile), f32),
                vmem((count, 2, 8, tile), f32),
                vmem((count, 8, tile), f32),
                vmem((count, 8, tile), f32),
                vmem((count, 2, tile, width), bf16),
                vmem((count, 2, tile, width), bf16),
            ]
            + [vmem((rows, wide), bf16)] * 2
            + [vmem((rows, channels), bf16)] * 6
            + [
                vmem((tiles, rows + 8, LANES), f32),
                vmem((tiles, rows + 16, LANES), f32),
                vmem((tiles, rows, LANES), f32),
                vmem((span, LANES), f32),
                vmem((span, 8, LANES), f32),
                vmem((groups, span), f32),
                vmem((n, share, span), f32),
                vmem((tp, share, span), f32),
                vmem((n * rows, tile), f32),
                vmem((width, tile), f32),
            ]
            + [vmem((2, tile, width), f32)] * 2
            + [vmem((count, tile, width), bf16)] * 3
            + [
                dma((6,)),
                dma((4, CHIPS, 2)),
                dma((4, CHIPS, count)),
                dma((CHIPS, 2)),
                dma((n,)),
                dma((count, 2)),
                dma((count,)),
                dma((count,)),
                dma((count,)),
                dma((count,)),
                dma((count,)),
                dma,
                dma,
                dma((3,)),
                dma((3,)),
                dma((3,)),
                dma((n,)),
                dma((n,)),
                dma((tp,)),
                dma((tp,)),
                dma((n,)),
                dma((n,)),
            ]
        ),
        compiler_params=pltpu.CompilerParams(
            collective_id=0, has_side_effects=True, vmem_limit_bytes=67043328
        ),
    )(q_heads, k_heads, v_heads, grad_attn, attn_out, gate_q, feat_k, feat_v, grad_y, filters)
    return pl.pallas_call(
        finish,
        out_shape=small + large[:1] + large + last,
        in_specs=[anywhere] * 8,
        out_specs=[anywhere] * 7,
        scratch_shapes=(
            [vmem((rows, channels), bf16)] * 3
            + [vmem((rows, wide), bf16)] * 3
            + [vmem((rows, channels), bf16)] * 2
            + [vmem((groups, span), f32), dma((8,)), dma((7,))]
        ),
    )(grad_y, conv_out, *parts)


def local(*args):
    n, tp = (lax.axis_size("seq"), lax.axis_size("tp"))
    rows, wide = args[0].shape
    groups, span = args[10].shape
    fits = (
        HEADS // tp == n
        and n == 2 * CHIPS
        and tp > 1
        and rows == LANES
        and wide == n * LANES
        and span <= rows
        and span == LANES
        and LANES % groups == 0
        and groups % (8 * n) == 0
    )
    if fits:
        return tuple(local_heads(n, tp, *args))
    return local_ring(*args)


def solution(mesh):
    in_specs = (
        P("seq", "tp"),
        P("seq", "tp"),
        P("seq", "tp"),
        P("seq", "tp"),
        P("seq", "tp"),
        P("seq", "tp"),
        P("seq", "tp"),
        P("seq", "tp"),
        P("seq", "tp"),
        P("seq", "tp"),
        P(),
    )
    out_specs = (
        P("seq", "tp"),
        P("seq", "tp"),
        P("seq", "tp"),
        P("seq", "tp"),
        P("seq", "tp"),
        P("seq", "tp"),
        P(),
    )
    return jax.shard_map(local, mesh=mesh, in_specs=in_specs, out_specs=out_specs, check_vma=False)
```

```python
import functools

import jax
import jax.numpy as jnp
from jax import lax
from jax.experimental import pallas as pl
from jax.experimental.pallas import tpu as pltpu
from jax.sharding import PartitionSpec as P

HEADS = 32


def from_behind(value, axis, steps):
    count = lax.axis_size(axis)
    leading, last = (max(0, -steps), min(count, count - steps))
    return lax.ppermute(value, axis, [(source, source + steps) for source in range(leading, last)])


def wire_parts(x):
    high = x.astype(jnp.bfloat16)
    back = lax.optimization_barrier(high).astype(jnp.float32)
    low = (x - back).astype(jnp.bfloat16)
    return (high, low)


def local_ring(
    q_heads,
    k_heads,
    v_heads,
    grad_attn,
    attn_out,
    gate_q,
    feat_k,
    feat_v,
    conv_out,
    grad_y,
    filters,
):
    rows = q_heads.shape[0]
    heads_here = HEADS // lax.axis_size("tp")
    width = q_heads.shape[1] // heads_here
    scale = 1.0 / width**0.5
    shards = lax.axis_size("seq")
    place = lax.axis_index("seq")
    queries = q_heads.reshape(rows, heads_here, width)
    upstream = grad_attn.reshape(rows, heads_here, width)
    keys_here = k_heads.reshape(rows, heads_here, width)
    values_here = v_heads.reshape(rows, heads_here, width)
    delta = jnp.sum(
        upstream.astype(jnp.float32)
        * attn_out.reshape(rows, heads_here, width).astype(jnp.float32),
        axis=2,
    )
    delta_heads = delta.T
    diagonal = jnp.arange(rows)[:, None] >= jnp.arange(rows)[None, :]

    def query_tile(state, key_piece, value_piece, live):
        top, total, acc = state
        count = key_piece.shape[0]
        key_block = key_piece.reshape(count, heads_here, width)
        value_block = value_piece.reshape(count, heads_here, width)
        scores = (
            jnp.einsum("qhd,khd->hqk", queries, key_block, preferred_element_type=jnp.float32)
            * scale
        )
        top_new = jnp.maximum(top, jnp.max(jnp.where(live[None], scores, -1e30), axis=2))
        weights = jnp.where(live[None], jnp.exp(scores - top_new[:, :, None]), 0.0)
        decay = jnp.exp(top - top_new)
        dprob = jnp.einsum(
            "qhd,khd->hqk", upstream, value_block, preferred_element_type=jnp.float32
        )
        term = jnp.einsum(
            "hqk,khd->qhd",
            weights * (dprob - delta_heads[:, :, None]),
            key_block.astype(jnp.float32),
            precision=lax.Precision.HIGHEST,
        )
        return (top_new, total * decay + jnp.sum(weights, axis=2), acc * decay.T[:, :, None] + term)

    zero_rows = jnp.zeros((rows, heads_here, width), jnp.float32)
    state = (
        jnp.full((heads_here, rows), -1e30, jnp.float32),
        jnp.zeros((heads_here, rows), jnp.float32),
        zero_rows,
    )
    state = query_tile(state, k_heads, v_heads, diagonal)

    def relay_keys(back, carry):
        inner, moving = carry
        moving = from_behind((moving[0], moving[1]), "seq", 1)
        valid = place >= back
        live = jnp.broadcast_to(valid, (rows, rows))
        inner = query_tile(inner, moving[0], moving[1], live)
        return (inner, moving)

    state, moved = lax.fori_loop(1, shards, relay_keys, (state, (k_heads, v_heads)))
    top, total, acc = state
    lse = (top + jnp.log(total)).T
    grad_query = acc * (1.0 / total).T[:, :, None] * scale
    lse_high, lse_low = wire_parts(lse)
    delta_high, delta_low = wire_parts(delta)
    stats = jnp.stack([lse_high, lse_low, delta_high, delta_low], axis=1)

    def key_tile(inner, query_piece, upstream_piece, stat_piece, live):
        key_grad, value_grad = inner
        count = query_piece.shape[0]
        query_block = query_piece.reshape(count, heads_here, width)
        upstream_block = upstream_piece.reshape(count, heads_here, width)
        lse_w = stat_piece[:, 0].astype(jnp.float32) + stat_piece[:, 1].astype(jnp.float32)
        delta_w = stat_piece[:, 2].astype(jnp.float32) + stat_piece[:, 3].astype(jnp.float32)
        scores = (
            jnp.einsum("qhd,khd->hqk", query_block, keys_here, preferred_element_type=jnp.float32)
            * scale
        )
        probs = jnp.where(live[None], jnp.exp(scores - lse_w.T[:, :, None]), 0.0)
        dprob = jnp.einsum(
            "qhd,khd->hqk", upstream_block, values_here, preferred_element_type=jnp.float32
        )
        dscore = probs * (dprob - delta_w.T[:, :, None])
        value_grad = value_grad + jnp.einsum(
            "hqk,qhd->khd",
            probs.astype(jnp.bfloat16),
            upstream_block,
            preferred_element_type=jnp.float32,
        )
        key_grad = key_grad + jnp.einsum(
            "hqk,qhd->khd",
            dscore.astype(jnp.bfloat16),
            query_block,
            preferred_element_type=jnp.float32,
        )
        return (key_grad, value_grad)

    grads = (zero_rows, zero_rows)
    grads = key_tile(grads, q_heads, grad_attn, stats, diagonal)

    def relay_queries(back, carry):
        inner, moving = carry
        moving = from_behind((moving[0], moving[1], moving[2]), "seq", -1)
        valid = place + back <= shards - 1
        live = jnp.broadcast_to(valid, (rows, rows))
        inner = key_tile(inner, moving[0], moving[1], moving[2], live)
        return (inner, moving)

    grads, moved = lax.fori_loop(1, shards, relay_queries, (grads, (q_heads, grad_attn, stats)))
    key_grad, value_grad = grads
    grad_q = grad_query.astype(jnp.bfloat16).reshape(rows, heads_here * width)
    grad_k = (key_grad * scale).astype(jnp.bfloat16).reshape(rows, heads_here * width)
    grad_v = value_grad.astype(jnp.bfloat16).reshape(rows, heads_here * width)
    span_taps = filters.shape[1]
    groups = filters.shape[0]
    channels = gate_q.shape[1]
    dz = (grad_y.astype(jnp.float32) * gate_q.astype(jnp.float32)).astype(jnp.bfloat16)
    rim = from_behind(dz[: span_taps - 1], "seq", -1)
    grad_gate = (grad_y.astype(jnp.float32) * conv_out.astype(jnp.float32)).astype(jnp.bfloat16)
    padded = jnp.concatenate([dz, rim], axis=0).astype(jnp.float32)
    taps = jnp.tile(filters.T, (1, channels // groups))
    mixed = feat_k.astype(jnp.float32) * feat_v.astype(jnp.float32)
    numbers = ("NWC", "WIO", "NWC")
    dw = lax.conv_general_dilated(
        padded[None],
        taps[:, None, :],
        (1,),
        "VALID",
        dimension_numbers=numbers,
        feature_group_count=channels,
        precision=lax.Precision.HIGHEST,
    )[0]
    local_terms = lax.conv_general_dilated(
        padded[None],
        mixed[:, None, :],
        (1,),
        "VALID",
        dimension_numbers=numbers,
        feature_group_count=channels,
        precision=lax.Precision.HIGHEST,
    )[0]
    grad_feat_k = (dw * feat_v.astype(jnp.float32)).astype(jnp.bfloat16)
    grad_feat_v = (dw * feat_k.astype(jnp.float32)).astype(jnp.bfloat16)
    local_terms = jnp.sum(local_terms.reshape(span_taps, channels // groups, groups), axis=1).T
    filter_total = lax.psum(local_terms, ("seq", "tp"))
    count_all = rows * shards * channels * lax.axis_size("tp") / groups
    grad_filters = filter_total * (1.0 / count_all**0.5)
    return (grad_q, grad_k, grad_v, grad_gate, grad_feat_k, grad_feat_v, grad_filters)


MESH = pl.DeviceIdType.MESH
LANES = 128
LOG2E = 1.4426950408889634
CHIPS = 4
CROSS = {0: ((1, 2), (1, 1), (2, 2), (2, 1)), 1: ((1, 2), (2, 2)), 2: ((0, 1), (3, 1)), 3: ((0, 2), (0, 1), (3, 2), (3, 1))}
DELTAS = {2: (1,), 3: (2, 1)}


def kernel(
    n,
    tp,
    q_in,
    k_in,
    v_in,
    do_in,
    ao_in,
    gate_in,
    fk_in,
    fv_in,
    gy_in,
    filters,
    gq_out,
    gk_out,
    gv_out,
    gfk_out,
    gfv_out,
    gf_out,
    heads_q,
    heads_k,
    heads_v,
    heads_do,
    keys_t,
    delta_mine,
    delta_all,
    lse_mine,
    lse_in,
    edge_mine,
    edge_in,
    part_mine,
    part_in,
    do_here,
    ao_here,
    gate,
    fk,
    fv,
    gy,
    dz_here,
    dz_rim,
    dz_all,
    rim_all,
    dw_all,
    taps,
    terms,
    partial_mine,
    partial_in,
    across,
    scores,
    grad_t,
    acc_k,
    acc_v,
    res_q,
    res_k,
    res_v,
    load_sem,
    send_x,
    recv_x,
    send_d,
    recv_d,
    send_l,
    recv_l,
    send_e,
    recv_e,
    send_p,
    recv_p,
    send_rim,
    recv_rim,
    send_out,
    recv_out,
    own_out,
    send_rs,
    recv_rs,
    send_tp,
    recv_tp,
    send_ag,
    recv_ag,
):
    me = lax.axis_index("seq")
    lane = lax.axis_index("tp")
    z = lax.div(me, 2)
    core = lax.rem(me, 2)
    other = 1 - core
    partner = 2 * z + other
    rows, width = q_in.shape[0], LANES
    count = q_in.shape[1] // width // 2
    half = count * width
    tile = 2 * rows
    channels = gy_in.shape[1]
    span = filters.shape[1]
    scale = 1.0 / width**0.5

    def chunk(i, size):
        return pl.ds(pl.multiple_of(i * size, size), size)

    def remote(src, dst, send, recv, device):
        return pltpu.make_async_remote_copy(
            src_ref=src,
            dst_ref=dst,
            send_sem=send,
            recv_sem=recv,
            device_id={"seq": device},
            device_id_type=MESH,
        )

    loads = [
        pltpu.make_async_copy(src, dst, load_sem.at[i])
        for i, (src, dst) in enumerate(
            (
                (do_in, do_here),
                (ao_in, ao_here),
                (gy_in, gy),
                (gate_in, gate),
                (fk_in, fk),
                (fv_in, fv),
            )
        )
    ]
    for load in loads:
        load.start()

    barrier = pltpu.get_barrier_semaphore()
    for d in range(1, n):
        pl.semaphore_signal(
            barrier, inc=1, device_id={"seq": lax.rem(me + d, n)}, device_id_type=MESH
        )
    for d in range(1, tp):
        pl.semaphore_signal(
            barrier, inc=1, device_id={"tp": lax.rem(lane + d, tp)}, device_id_type=MESH
        )
    pl.semaphore_wait(barrier, n - 1 + tp - 1)

    ins = (q_in, k_in, v_in, do_in)
    heads = (heads_q, heads_k, heads_v, heads_do)

    def move(a, h, chip, to):
        return remote(
            ins[a].at[:, chunk(to * count + h, width)],
            heads[a].at[h, chunk(me, rows), :],
            send_x.at[a, chip, to],
            recv_x.at[a, z, h],
            2 * chip + to,
        )

    def moved(a, chip, to):
        return remote(
            ins[a].at[:, chunk(to, half)],
            ins[a].at[:, chunk(to, half)],
            send_x.at[a, chip, to],
            recv_x.at[a, chip, 0],
            2 * chip + to,
        )

    def own(a, h):
        return pltpu.make_async_copy(
            ins[a].at[:, chunk(core * count + h, width)],
            heads[a].at[h, chunk(me, rows), :],
            recv_x.at[a, z, h],
        )

    def arrive(a, chip, h):
        at = heads[a].at[h, chunk(chip, tile), :]
        remote(at, at, send_x.at[a, 0, 0], recv_x.at[a, chip, h], partner).wait_recv()

    def exchange(h):
        for a in (0, 1, 3, 2):
            own(a, h).start()
            move(a, h, z, other).start()

    def outward(h):
        for chip in range(CHIPS):

            @pl.when(z == chip)
            def _():
                for a, to in CROSS[chip]:
                    for side in range(2):
                        move(a, h, to, side).start()

    def rim_copy():
        return remote(dz_here, dz_rim, send_rim, recv_rim, lax.rem(me + n - 1, n))

    def delta_copy(chip, to):
        return remote(
            delta_mine.at[to],
            delta_all.at[me],
            send_d.at[chip, to],
            recv_d.at[me],
            2 * chip + to,
        )

    def delta_wait(chip):
        for side in range(2):
            b = 2 * chip + side
            at = delta_all.at[b]

            @pl.when(b != me)
            def _():
                remote(at, at, send_d.at[0, 0], recv_d.at[b], partner).wait_recv()

    for h in range(count):
        exchange(h)
    outward(0)

    loads[0].wait()
    loads[1].wait()
    for h in range(2 * count):
        at = slice(h * width, (h + 1) * width)
        prod = do_here[:, at].astype(jnp.float32) * ao_here[:, at].astype(jnp.float32)
        line = jnp.sum(prod.T, axis=0, keepdims=True)
        delta_mine[h // count, h % count] = jnp.broadcast_to(line, (8, rows))
    delta_all[me] = delta_mine[core]
    delta_copy(z, other).start()
    for chip, targets in DELTAS.items():

        @pl.when(z == chip)
        def _():
            for to in targets:
                for side in range(2):
                    delta_copy(to, side).start()

    key_id = lax.broadcasted_iota(jnp.int32, (tile, tile), 0)
    query_id = lax.broadcasted_iota(jnp.int32, (tile, tile), 1)
    nt = (((1,), (1,)), ((), ()))
    nn = (((1,), (0,)), ((), ()))

    def dot(a, b, dims):
        return lax.dot_general(a, b, dims, preferred_element_type=jnp.float32)

    def at_tile(i):
        return slice(i * tile, (i + 1) * tile)

    def log_sums(h, i, keys):
        query = heads_q[h, at_tile(i), :]
        top = None
        for j in keys:
            raw = dot(heads_k[h, at_tile(j), :], query, nt)
            if j == i:
                raw = jnp.where(key_id <= query_id, raw, -1e30)
            scores[at_tile(j), :] = raw
            high = jnp.max(raw, axis=0, keepdims=True)
            top = high if top is None else jnp.maximum(top, high)
        total = jnp.zeros_like(top)
        for j in keys:
            weight = jnp.exp2((scores[at_tile(j), :] - top) * (scale * LOG2E))
            total = total + jnp.sum(weight, axis=0, keepdims=True)
        return top * scale + jnp.log(total)

    def wire(x):
        high = x.astype(jnp.bfloat16).astype(jnp.float32)
        return high + (x - high).astype(jnp.bfloat16).astype(jnp.float32)

    def delta_row(h, i):
        return jnp.concatenate(
            [delta_all[2 * i, h][0:1, :], delta_all[2 * i + 1, h][0:1, :]], axis=1
        )

    def turn_keys(h, j):
        keys_t[:, at_tile(j)] = heads_k[h, at_tile(j), :].T

    def pair(h, i, j, lse, want_q, want_k, fresh_q=False, fresh_k=False):
        query = heads_q[h, at_tile(i), :]
        upstream = heads_do[h, at_tile(i), :]
        delta = delta_row(h, i)
        lse_w = wire(lse)
        base = lse if want_q else lse_w
        raw = dot(heads_k[h, at_tile(j), :], query, nt)
        prob = jnp.exp2(raw * (scale * LOG2E) - base * LOG2E)
        if i == j:
            prob = jnp.where(key_id <= query_id, prob, 0.0)
        dprob = dot(heads_v[h, at_tile(j), :], upstream, nt)
        if want_q:
            dscore = prob * (dprob - delta)
            big = dscore.astype(jnp.bfloat16)
            rest = (dscore - big.astype(jnp.float32)).astype(jnp.bfloat16)
            turned = keys_t[:, at_tile(j)]
            grad = dot(turned, big, nn) + dot(turned, rest, nn)
            grad_t[...] = grad if fresh_q else grad_t[...] + grad
        if want_k:
            prob_k = prob * jnp.exp(lse - lse_w) if want_q else prob
            dscore_k = (prob_k * (dprob - wire(delta))).astype(jnp.bfloat16)
            grad_v = dot(prob_k.astype(jnp.bfloat16), upstream, nn)
            grad_k = dot(dscore_k, query, nn)
            acc_v[j % 2] = grad_v if fresh_k else acc_v[j % 2] + grad_v
            acc_k[j % 2] = grad_k if fresh_k else acc_k[j % 2] + grad_k

    results = ((res_q, gq_out), (res_k, gk_out), (res_v, gv_out))

    def give(a, h):
        src, dst = results[a]
        at = chunk(core * count + h, width)
        pltpu.make_async_copy(
            src.at[h, chunk(core, rows), :], dst.at[:, at], own_out.at[a]
        ).start()
        remote(
            src.at[h, chunk(other, rows), :],
            dst.at[:, at],
            send_out.at[a],
            recv_out.at[a],
            partner,
        ).start()

    def lse_copy(h, chip):
        if chip == 1:
            return remote(
                lse_mine.at[h], lse_in.at[h], send_l.at[h, 0], recv_l.at[h], 2 * chip + core
            )
        return remote(
            lse_mine.at[h, 1], lse_in.at[h, 1], send_l.at[h, 1], recv_l.at[h], 2 * chip + core
        )

    def edge_copy(h):
        return remote(
            edge_mine.at[h], edge_in.at[h], send_e.at[h], recv_e.at[h], 2 * 2 + core
        )

    def part_copy(h, chip):
        if chip == 0:
            return remote(
                part_mine.at[h], part_in.at[h], send_p.at[h], recv_p.at[h], 2 * chip + core
            )
        return remote(
            part_mine.at[h, 0], part_in.at[h, 0], send_p.at[h], recv_p.at[h], 2 * chip + core
        )

    def spread(row):
        return jnp.broadcast_to(row, (8, tile))

    def later_sums(h):
        for a, chip in ((0, 2), (1, 2), (1, 0), (1, 1), (0, 3)):
            arrive(a, chip, h)
        edge_copy(h).wait_recv()
        lse_mine[h, 0] = spread(log_sums(h, 2, (0, 1, 2)))
        near = log_sums(h, 3, (0, 1, 2))
        far = edge_in[h][0:1, :]
        top = jnp.maximum(near, far)
        lse_mine[h, 1] = spread(top + jnp.log(jnp.exp(near - top) + jnp.exp(far - top)))
        lse_copy(h, 1).start()
        lse_copy(h, 3).start()

        @pl.when(h < count - 2)
        def _():
            outward(h + 2)

    def head_first(h):
        for a in range(4):
            arrive(a, 0, h)
        turn_keys(h, 0)
        pair(h, 0, 0, log_sums(h, 0, (0,)), True, True, True, True)
        res_q[h] = (grad_t[...] * scale).T.astype(jnp.bfloat16)
        give(0, h)
        part_copy(h, 0).wait_recv()
        res_k[h] = ((acc_k[0] + part_in[h, 0].astype(jnp.float32)) * scale).astype(jnp.bfloat16)
        res_v[h] = (acc_v[0] + part_in[h, 1].astype(jnp.float32)).astype(jnp.bfloat16)
        give(1, h)
        give(2, h)

    def head_second(h):
        for a in range(4):
            arrive(a, 1, h)
        arrive(1, 0, h)
        lse = log_sums(h, 1, (0, 1))
        turn_keys(h, 0)
        turn_keys(h, 1)
        arrive(2, 0, h)
        pair(h, 1, 0, lse, True, True, True, True)
        pair(h, 1, 1, lse, True, True, False, True)
        res_q[h] = (grad_t[...] * scale).T.astype(jnp.bfloat16)
        give(0, h)
        lse_copy(h, 1).wait_recv()
        for i in (2, 3):
            arrive(0, i, h)
            arrive(3, i, h)
            pair(h, i, 0, lse_in[h, i - 2][0:1, :], False, True)
            if i == 3:
                part_mine[h, 0] = acc_k[0].astype(jnp.bfloat16)
                part_mine[h, 1] = acc_v[0].astype(jnp.bfloat16)
                part_copy(h, 0).start()
            pair(h, i, 1, lse_in[h, i - 2][0:1, :], False, True)
        res_k[h] = (acc_k[1] * scale).astype(jnp.bfloat16)
        res_v[h] = acc_v[1].astype(jnp.bfloat16)
        give(1, h)
        give(2, h)

    def head_third(h):
        later_sums(h)
        for j in range(3):
            turn_keys(h, j)
        for a, chip in ((2, 2), (3, 2), (2, 0), (2, 1), (3, 3)):
            arrive(a, chip, h)
        lse = lse_mine[h, 1][0:1, :]
        pair(h, 3, 0, lse, True, False, True)
        pair(h, 3, 1, lse, True, False)
        pair(h, 3, 2, lse, True, True, False, True)
        part_mine[h, 0] = grad_t[...].T.astype(jnp.bfloat16)
        part_copy(h, 3).start()
        lse = lse_mine[h, 0][0:1, :]
        pair(h, 2, 0, lse, True, False, True)
        pair(h, 2, 1, lse, True, False)
        pair(h, 2, 2, lse, True, True)
        res_q[h] = (grad_t[...] * scale).T.astype(jnp.bfloat16)
        res_k[h] = (acc_k[0] * scale).astype(jnp.bfloat16)
        res_v[h] = acc_v[0].astype(jnp.bfloat16)
        for a in range(3):
            give(a, h)

    def head_last(h):
        for a in (2, 3):
            arrive(a, 3, h)
        lse_copy(h, 3).wait_recv()
        turn_keys(h, 3)
        pair(h, 3, 3, lse_in[h, 1][0:1, :], True, True, True, True)
        res_k[h] = (acc_k[1] * scale).astype(jnp.bfloat16)
        res_v[h] = acc_v[1].astype(jnp.bfloat16)
        give(1, h)
        give(2, h)
        part_copy(h, 3).wait_recv()
        total = grad_t[...].T + part_in[h, 0].astype(jnp.float32)
        res_q[h] = (total * scale).astype(jnp.bfloat16)
        give(0, h)

    @pl.when(z == 3)
    def _():
        def edge(h, carry):
            arrive(0, 3, h)
            arrive(1, 3, h)
            edge_mine[h] = spread(log_sums(h, 3, (3,)))
            edge_copy(h).start()
            return carry

        lax.fori_loop(0, count, edge, 0)

    loads[2].wait()
    loads[3].wait()
    tiles = channels // LANES
    for t in range(tiles):
        at = slice(t * LANES, (t + 1) * LANES)
        dz = (gy[:, at].astype(jnp.float32) * gate[:, at].astype(jnp.float32)).astype(jnp.bfloat16)
        dz_here[:, at] = dz
        dz_all[t, 0:rows, :] = dz.astype(jnp.float32)
        dz_all[t, rows : rows + 8, :] = jnp.zeros((8, LANES), jnp.float32)

    @pl.when(me > 0)
    def _():
        rim_copy().start()

    outward(1)

    @pl.when(z != 2)
    def _():
        outward(2)

    @pl.when(z < 2)
    def _():
        outward(count - 1)

    for chip in range(CHIPS):

        @pl.when(z == chip)
        def _():
            delta_wait(chip)

    loads[4].wait()
    loads[5].wait()
    terms[...] = jnp.zeros_like(terms)
    both = jnp.concatenate([filters[...]] * (LANES // filters.shape[0]), axis=0)
    taps[...] = both.T

    def conv_own(t, carry):
        at = pl.ds(pl.multiple_of(t * LANES, LANES), LANES)
        mixed = fk[:, at].astype(jnp.float32) * fv[:, at].astype(jnp.float32)
        for a in range(span // 8):
            size = rows - 8 * a
            part = None
            for b in range(8):
                tap = 8 * a + b
                x = dz_all[t, tap : tap + size, :]
                term = x * taps[tap : tap + 1, :]
                part = term if part is None else part + term
                prod = (x * mixed[0:size]).reshape(size // 8, 8, LANES)
                terms[tap] = terms[tap] + jnp.sum(prod, axis=0)
            if a == 0:
                dw_all[t] = part
            else:
                dw_all[t, 0:size, :] = dw_all[t, 0:size, :] + part
        return carry

    lax.fori_loop(0, tiles, conv_own, 0)

    @pl.when(z == 1)
    def _():
        delta_wait(2)
        delta_wait(3)

    @pl.when(z == 2)
    def _():
        delta_wait(3)

    def rim_part():
        @pl.when(me < n - 1)
        def _():
            rim_copy().wait_recv()
            for t in range(tiles):
                at = slice(t * LANES, (t + 1) * LANES)
                rim_all[t, 0:8, :] = jnp.zeros((8, LANES), jnp.float32)
                rim_all[t, 8 : rows + 8, :] = dz_rim[:, at].astype(jnp.float32)

        @pl.when(me == n - 1)
        def _():
            for t in range(tiles):
                rim_all[t, 0 : rows + 8, :] = jnp.zeros((rows + 8, LANES), jnp.float32)

        def conv_rim(t, carry):
            at = pl.ds(pl.multiple_of(t * LANES, LANES), LANES)
            left = fk[:, at].astype(jnp.float32)
            right = fv[:, at].astype(jnp.float32)
            mixed = left * right
            for a in range(span // 8):
                size = 8 * (a + 1)
                part = None
                for b in range(8):
                    tap = 8 * a + b
                    x = rim_all[t, b : b + size, :]
                    term = x * taps[tap : tap + 1, :]
                    part = term if part is None else part + term
                    prod = (x * mixed[rows - size : rows]).reshape(size // 8, 8, LANES)
                    terms[tap] = terms[tap] + jnp.sum(prod, axis=0)
                dw_all[t, rows - size : rows, :] = dw_all[t, rows - size : rows, :] + part
            acc = dw_all[t]
            gfk_out[:, at] = (acc * right).astype(jnp.bfloat16)
            gfv_out[:, at] = (acc * left).astype(jnp.bfloat16)
            return carry

        lax.fori_loop(0, tiles, conv_rim, 0)
    share = gf_out.shape[0] // n

    def slab(i):
        return chunk(i, share)

    def seq_copy(d):
        peer = lax.rem(me + d, n)
        return remote(
            partial_mine.at[slab(peer), :], partial_in.at[me], send_rs.at[d], recv_rs.at[d], peer
        )

    def tp_copy(d):
        return pltpu.make_async_remote_copy(
            src_ref=across.at[lane],
            dst_ref=across.at[lane],
            send_sem=send_tp.at[d],
            recv_sem=recv_tp.at[d],
            device_id={"tp": lax.rem(lane + d, tp)},
            device_id_type=MESH,
        )

    def all_copy(d):
        at = gf_out.at[slab(me), :]
        return remote(at, at, send_ag.at[d], recv_ag.at[d], lax.rem(me + d, n))

    def sum_here():
        per_lane = jnp.sum(terms[...], axis=1)
        groups = gf_out.shape[0]
        folded = per_lane
        for g in range(1, LANES // groups):
            folded = folded + pltpu.roll(per_lane, g * groups, 1)
        partial_mine[...] = folded.T[0:groups, :]
        partial_in[me] = partial_mine[slab(me), :]
        for d in range(1, n):
            seq_copy(d).start()

    def sum_seq():
        for d in range(1, n):
            seq_copy(d).wait_recv()
        total = partial_in[0]
        for i in range(1, n):
            total = total + partial_in[i]
        across[lane] = total
        for d in range(1, tp):
            tp_copy(d).start()

    def sum_tp():
        for d in range(1, tp):
            tp_copy(d).wait_recv()
        total = across[0]
        for i in range(1, tp):
            total = total + across[i]
        count_all = rows * n * channels * tp / gf_out.shape[0]
        gf_out[slab(me), :] = total * (1.0 / count_all**0.5)
        for d in range(1, n):
            all_copy(d).start()

    def per_head(h, carry):
        @pl.when(h == 0)
        def _():
            rim_part()
            sum_here()

            @pl.when(z == 3)
            def _():
                outward(count - 1)

        @pl.when(h == count - 2)
        def _():
            sum_seq()

        @pl.when(h == count - 1)
        def _():
            sum_tp()

        for chip, work in enumerate((head_first, head_second, head_third, head_last)):

            @pl.when(z == chip)
            def _():
                work(h)

        return carry

    lax.fori_loop(0, count, per_head, 0)

    @pl.when(me > 0)
    def _():
        rim_copy().wait_send()

    for a in range(4):
        moved(a, z, other).wait_send()
    delta_copy(z, other).wait_send()
    for chip in range(CHIPS):

        @pl.when(z == chip)
        def _():
            for a, to in CROSS[chip]:
                for side in range(2):
                    moved(a, to, side).wait_send()
            for to in DELTAS.get(chip, ()):
                for side in range(2):
                    delta_copy(to, side).wait_send()
            for h in range(count):
                if chip == 1:
                    part_copy(h, 0).wait_send()
                if chip == 2:
                    part_copy(h, 3).wait_send()
                    lse_copy(h, 1).wait_send()
                    lse_copy(h, 3).wait_send()
                if chip == 3:
                    edge_copy(h).wait_send()

    for a in range(3):
        dst = results[a][1]
        mine = dst.at[:, chunk(core, half)]
        theirs = dst.at[:, chunk(other, half)]
        pltpu.make_async_copy(mine, mine, own_out.at[a]).wait()
        remote(theirs, theirs, send_out.at[a], recv_out.at[a], partner).wait()
    for d in range(1, n):
        seq_copy(d).wait_send()
        all_copy(d).wait()
    for d in range(1, tp):
        tp_copy(d).wait_send()


def finish(
    gy_in,
    co_in,
    gq_in,
    gk_in,
    gv_in,
    gfk_in,
    gfv_in,
    gf_in,
    gq_out,
    gk_out,
    gv_out,
    gg_out,
    gfk_out,
    gfv_out,
    gf_out,
    gy,
    co,
    gg,
    gq,
    gk,
    gv,
    gfk,
    gfv,
    gf,
    sem_in,
    sem_out,
):
    sources = (gy_in, co_in, gq_in, gk_in, gv_in, gfk_in, gfv_in, gf_in)
    holds = (gy, co, gq, gk, gv, gfk, gfv, gf)
    taken = [
        pltpu.make_async_copy(src, dst, sem_in.at[i])
        for i, (src, dst) in enumerate(zip(sources, holds))
    ]
    for copy in taken:
        copy.start()
    given = []

    def give(src, dst):
        copy = pltpu.make_async_copy(src, dst, sem_out.at[len(given)])
        copy.start()
        given.append(copy)

    outs = (gq_out, gk_out, gv_out, gfk_out, gfv_out, gf_out)
    taken[0].wait()
    taken[1].wait()
    gg[...] = (gy[...].astype(jnp.float32) * co[...].astype(jnp.float32)).astype(jnp.bfloat16)
    give(gg, gg_out)
    for i, dst in enumerate(outs):
        taken[2 + i].wait()
        give(holds[2 + i], dst)
    for copy in given:
        copy.wait()


def local_heads(
    n,
    tp,
    q_heads,
    k_heads,
    v_heads,
    grad_attn,
    attn_out,
    gate_q,
    feat_k,
    feat_v,
    conv_out,
    grad_y,
    filters,
):
    rows, wide = q_heads.shape
    width = LANES
    count = wide // width // 2
    tile = 2 * rows
    channels = gate_q.shape[1]
    groups, span = filters.shape
    share = groups // n
    tiles = channels // LANES
    bf16, f32 = (jnp.bfloat16, jnp.float32)
    anywhere = pl.BlockSpec(memory_space=pl.ANY)
    inside = pl.BlockSpec(memory_space=pltpu.VMEM)
    dma = pltpu.SemaphoreType.DMA
    vmem = pltpu.VMEM
    small = [jax.ShapeDtypeStruct((rows, wide), bf16)] * 3
    large = [jax.ShapeDtypeStruct((rows, channels), bf16)] * 2
    last = [jax.ShapeDtypeStruct((groups, span), f32)]
    parts = pl.pallas_call(
        functools.partial(kernel, n, tp),
        out_shape=small + large + last,
        in_specs=[anywhere] * 9 + [inside],
        out_specs=[anywhere] * 3 + [inside] * 3,
        scratch_shapes=(
            [vmem((count, n * rows, width), bf16)] * 4
            + [
                vmem((width, n * rows), bf16),
                vmem((2, count, 8, rows), f32),
                vmem((n, count, 8, rows), f32),
                vmem((count, 2, 8, tile), f32),
                vmem((count, 2, 8, tile), f32),
                vmem((count, 8, tile), f32),
                vmem((count, 8, tile), f32),
                vmem((count, 2, tile, width), bf16),
                vmem((count, 2, tile, width), bf16),
            ]
            + [vmem((rows, wide), bf16)] * 2
            + [vmem((rows, channels), bf16)] * 6
            + [
                vmem((tiles, rows + 8, LANES), f32),
                vmem((tiles, rows + 16, LANES), f32),
                vmem((tiles, rows, LANES), f32),
                vmem((span, LANES), f32),
                vmem((span, 8, LANES), f32),
                vmem((groups, span), f32),
                vmem((n, share, span), f32),
                vmem((tp, share, span), f32),
                vmem((n * rows, tile), f32),
                vmem((width, tile), f32),
            ]
            + [vmem((2, tile, width), f32)] * 2
            + [vmem((count, tile, width), bf16)] * 3
            + [
                dma((6,)),
                dma((4, CHIPS, 2)),
                dma((4, CHIPS, count)),
                dma((CHIPS, 2)),
                dma((n,)),
                dma((count, 2)),
                dma((count,)),
                dma((count,)),
                dma((count,)),
                dma((count,)),
                dma((count,)),
                dma,
                dma,
                dma((3,)),
                dma((3,)),
                dma((3,)),
                dma((n,)),
                dma((n,)),
                dma((tp,)),
                dma((tp,)),
                dma((n,)),
                dma((n,)),
            ]
        ),
        compiler_params=pltpu.CompilerParams(
            collective_id=0, has_side_effects=True, vmem_limit_bytes=67043328
        ),
    )(q_heads, k_heads, v_heads, grad_attn, attn_out, gate_q, feat_k, feat_v, grad_y, filters)
    return pl.pallas_call(
        finish,
        out_shape=small + large[:1] + large + last,
        in_specs=[anywhere] * 8,
        out_specs=[anywhere] * 7,
        scratch_shapes=(
            [vmem((rows, channels), bf16)] * 3
            + [vmem((rows, wide), bf16)] * 3
            + [vmem((rows, channels), bf16)] * 2
            + [vmem((groups, span), f32), dma((8,)), dma((7,))]
        ),
    )(grad_y, conv_out, *parts)


def local(*args):
    n, tp = (lax.axis_size("seq"), lax.axis_size("tp"))
    rows, wide = args[0].shape
    groups, span = args[10].shape
    fits = (
        HEADS // tp == n
        and n == 2 * CHIPS
        and tp > 1
        and rows == LANES
        and wide == n * LANES
        and span <= rows
        and span == LANES
        and LANES % groups == 0
        and groups % (8 * n) == 0
    )
    if fits:
        return tuple(local_heads(n, tp, *args))
    return local_ring(*args)


def solution(mesh):
    in_specs = (
        P("seq", "tp"),
        P("seq", "tp"),
        P("seq", "tp"),
        P("seq", "tp"),
        P("seq", "tp"),
        P("seq", "tp"),
        P("seq", "tp"),
        P("seq", "tp"),
        P("seq", "tp"),
        P("seq", "tp"),
        P(),
    )
    out_specs = (
        P("seq", "tp"),
        P("seq", "tp"),
        P("seq", "tp"),
        P("seq", "tp"),
        P("seq", "tp"),
        P("seq", "tp"),
        P(),
    )
    return jax.shard_map(local, mesh=mesh, in_specs=in_specs, out_specs=out_specs, check_vma=False)
```
